512 devices in a mesh: gx: 32 (over y, z_hi, core), gy: 16 (over z_lo, x).
Axes of the slice: x: 4, y: 4, z: 16 (z_hi: 4, z_lo: 4; z = z_hi * 4 + z_lo), core: 2. Of those that a mesh axis runs over, the one named last changes fastest.
Arguments:
- features: bfloat16 [32, 16, 4, 6144], P('gx', 'gy'), may hold values from -6 to 6
- cotangent: bfloat16 [32, 16, 4, 6144], P('gx', 'gy'), may hold values from -6 to 6
- brick_slot: int32 [32, 16, 2, 2, 2], P('gx', 'gy'), may hold values from 0 to 4, as said below
- weight_one: bfloat16 [27, 96, 96], replicated, may hold values from -0.125 to 0.125
- weight_two: bfloat16 [27, 96, 96], replicated, may hold values from -0.125 to 0.125
- gain: float32 [96], replicated, may hold values from 0.1 to 1.9
- bias: float32 [96], replicated, may hold values from -0.5 to 0.5
Outputs:
- out: bfloat16 [32, 16, 4, 6144], P('gx', 'gy')
- grad_features: bfloat16 [32, 16, 4, 6144], P('gx', 'gy')
- grad_weight_one: float32 [27, 96, 96], replicated
- grad_weight_two: float32 [27, 96, 96], replicated
- grad_gain: float32 [96], replicated
- grad_bias: float32 [96], replicated
The draws below stay inside these ranges and needn't reach their ends.
Inputs may be any that keep to these rules, and one draw needn't show every extreme that they name: `brick_slot`: on each slab the values below 4 are the slots 0 to n - 1, each in exactly one cell, for some n from 2 to 4; all other cells hold 4. At least one slab has n = 4.
All inputs are finite; a program needn't handle non-finite values.
Results may differ from the reference program's by a relative error of at most 0.003.
Values may be sent and summed in bfloat16 or wider, within the bound.
No kernel may reach another device: no remote copies, remote signals or barrier semaphores. Data moves between devices by JAX's collectives and lax.ppermute only.
A program may use at most 64 MiB of HBM per device.

```python
import math
import jax
import jax.numpy as jnp
from jax import lax

C = 96
TAPS = 27
VOX = 64
BSIDE = 2
COLUMN = 2
CELLS = 8
NB = 4
SLABS_X = 32
SLABS_Y = 16


def draw_brick_slot(key, part):
    devices = SLABS_X * SLABS_Y
    key_count = jax.random.fold_in(key, 11)
    key_full = jax.random.fold_in(key, 23)
    key_order = jax.random.fold_in(key, 37)
    counts = jax.random.randint(key_count, (devices,), NB // 2, NB + 1)
    chosen = jax.random.randint(key_full, (), 0, devices)
    counts = jnp.where(jnp.arange(devices) == chosen, NB, counts)
    orders = jax.vmap(lambda one_key: jax.random.permutation(one_key, CELLS))(jax.random.split(key_order, devices))
    ranks = jnp.argsort(orders, axis=1)
    slots = jnp.where(ranks < counts[:, None], ranks, NB)
    return slots.reshape(SLABS_X, SLABS_Y, BSIDE, BSIDE, COLUMN).astype(jnp.int32)


def block_levels(own_key, extent, cuts, smallest, largest):
    def one(position, shards_of):
        steps = jax.random.uniform(jax.random.fold_in(jax.random.fold_in(own_key, 6), position), (shards_of,), jnp.float32, smallest / len(cuts), largest / len(cuts))
        return jnp.repeat(jnp.exp(steps), extent[position] // shards_of).reshape((-1,) + (1,) * (len(extent) - position - 1))

    level = one(*cuts[0])
    for cut in cuts[1:]:
        level = level * one(*cut)
    return level


def noise(rng, extent, scale, most, cuts=(), held_as=jnp.bfloat16):
    values = scale * jax.random.normal(rng, extent, jnp.float32)
    if cuts:
        values = values * block_levels(rng, extent, cuts, -0.22, 0.18)
    return jnp.clip(values, -most, most).astype(held_as)


def setup_inputs(seed: int = 0) -> dict:
    splits = jax.random.split(jax.random.key(seed), 8)
    return {
        "features": noise(splits[0], (SLABS_X, SLABS_Y, NB, VOX * C), 1.0, 6.0, ((0, 32), (1, 16))),
        "cotangent": noise(splits[1], (SLABS_X, SLABS_Y, NB, VOX * C), 1.0, 6.0, ((0, 32), (1, 16))),
        "brick_slot": draw_brick_slot(jax.random.fold_in(splits[7], 71), 0),
        "weight_one": noise(splits[3], (TAPS, C, C), (TAPS * C) ** -0.5, 0.125),
        "weight_two": noise(splits[4], (TAPS, C, C), (TAPS * C) ** -0.5, 0.125),
        "gain": jnp.clip(1.0 + 0.18 * jax.random.normal(splits[5], (C,), jnp.float32), 0.1, 1.9),
        "bias": jnp.clip(jax.random.uniform(splits[6], (C,), jnp.float32, -0.5, 0.5), -0.5, 0.5),
    }


def brick_layout(slot_cells, count_slots, cells_side, column):
    total_cells = slot_cells.shape[0]
    cell_ids = jnp.zeros((count_slots + 1,), jnp.int32).at[slot_cells].set(jnp.arange(total_cells, dtype=jnp.int32))[:count_slots]
    filled = jnp.sum((slot_cells < count_slots).astype(jnp.int32))
    live = (jnp.arange(count_slots, dtype=jnp.int32) < filled).astype(jnp.float32)
    cell_x = cell_ids // (cells_side * column)
    cell_y = cell_ids // column % cells_side
    cell_z = cell_ids % column
    return ((cell_x, cell_y, cell_z), live)

def assemble(ext_flat, cells, span_y, span_z):
    pieces_at = {-1: slice(3, 4), 0: slice(0, 4), 1: slice(0, 1)}
    planes = []
    for along_x in (-1, 0, 1):
        lines = []
        for along_y in (-1, 0, 1):
            blocks = []
            for along_z in (-1, 0, 1):
                rows_index = ((cells[0] + 1 + along_x) * span_y + cells[1] + 1 + along_y) * span_z + cells[2] + 1 + along_z
                whole_bricks = jnp.take(ext_flat, rows_index, axis=0)
                blocks.append(whole_bricks[:, pieces_at[along_x], pieces_at[along_y], pieces_at[along_z], :])
            lines.append(jnp.concatenate(blocks, axis=3))
        planes.append(jnp.concatenate(lines, axis=2))
    return jnp.concatenate(planes, axis=1)

def conv_taps(padded, kernel):
    channels = kernel.shape[1]
    total = jnp.zeros((padded.shape[0] * 64, channels), jnp.float32)
    for along_x in (-1, 0, 1):
        for along_y in (-1, 0, 1):
            for along_z in (-1, 0, 1):
                tap = 9 * (along_x + 1) + 3 * (along_y + 1) + (along_z + 1)
                window = padded[:, 1 + along_x:5 + along_x, 1 + along_y:5 + along_y, 1 + along_z:5 + along_z, :]
                total = total + jnp.dot(window.reshape(-1, channels), kernel[tap], preferred_element_type=jnp.float32)
    return total.reshape(padded.shape[0], 4, 4, 4, channels)

def weight_taps(padded, grads):
    channels = grads.shape[-1]
    flat_grads = grads.reshape(-1, channels)
    results = []
    for along_x in (-1, 0, 1):
        for along_y in (-1, 0, 1):
            for along_z in (-1, 0, 1):
                window = padded[:, 1 + along_x:5 + along_x, 1 + along_y:5 + along_y, 1 + along_z:5 + along_z, :]
                results.append(jnp.dot(window.reshape(-1, channels).T, flat_grads, preferred_element_type=jnp.float32))
    return jnp.stack(results, axis=0)

def flipped(kernel):
    return jnp.transpose(jnp.flip(kernel, 0), (0, 2, 1))

def reference(features, cotangent, brick_slot, weight_one, weight_two, gain, bias):
    devices = SLABS_X * SLABS_Y
    width = VOX * C
    slot_all = brick_slot.reshape(devices, CELLS)

    def global_grid(values):
        source = jnp.concatenate([values, jnp.zeros((devices, 1, width), values.dtype)], axis=1)
        grids = jax.vmap(lambda source_rows, cell_picks: jnp.take(source_rows, cell_picks, axis=0))(source, slot_all)
        grids = grids.reshape(SLABS_X, SLABS_Y, BSIDE, BSIDE, COLUMN, width)
        grids = grids.transpose(0, 2, 1, 3, 4, 5).reshape(SLABS_X * BSIDE, SLABS_Y * BSIDE, COLUMN, width)
        return jnp.pad(grids, ((1, 1), (1, 1), (1, 1), (0, 0)))

    def padded_at(whole, device):
        start_x = device // SLABS_Y * BSIDE
        start_y = device % SLABS_Y * BSIDE
        extended = lax.dynamic_slice(whole, (start_x, start_y, device * 0, device * 0), (BSIDE + 2, BSIDE + 2, COLUMN + 2, width))
        ext_flat = extended.reshape(-1, 4, 4, 4, C)
        cells, live = brick_layout(slot_all[device], NB, BSIDE, COLUMN)
        return (assemble(ext_flat, cells, BSIDE + 2, COLUMN + 2), live)

    def conv_all(values, kernel):
        whole = global_grid(values.reshape(devices, NB, width))

        def one_slab(device):
            padded, live = padded_at(whole, device)
            return conv_taps(padded, kernel) * live[:, None, None, None, None]
        return lax.map(one_slab, jnp.arange(devices, dtype=jnp.int32))

    def grads_all(values, grads):
        whole = global_grid(values.reshape(devices, NB, width))

        def add_slab(total, device):
            padded, live = padded_at(whole, device)
            return (total + weight_taps(padded, grads[device]), None)
        start = jnp.zeros((TAPS, C, C), jnp.float32)
        return lax.scan(add_slab, start, jnp.arange(devices, dtype=jnp.int32))[0]
    live_all = jax.vmap(lambda slot_cells: brick_layout(slot_cells, NB, BSIDE, COLUMN)[1])(slot_all)
    live_all = live_all[:, :, None, None, None, None]
    inputs = features.reshape(devices, NB, 4, 4, 4, C)
    upstream = cotangent.reshape(devices, NB, 4, 4, 4, C)
    first_conv = conv_all(inputs, weight_one)
    pre = first_conv * gain + bias
    hidden = (jax.nn.silu(pre) * live_all).astype(jnp.bfloat16)
    out = ((inputs.astype(jnp.float32) + conv_all(hidden, weight_two)) * live_all).astype(jnp.bfloat16)
    masked_cotangent = (upstream.astype(jnp.float32) * live_all).astype(jnp.bfloat16)
    grad_two = grads_all(hidden, masked_cotangent)
    back_hidden = conv_all(masked_cotangent, flipped(weight_two))
    sigmoid = jax.nn.sigmoid(pre)
    back_pre = back_hidden * (sigmoid * (1.0 + pre * (1.0 - sigmoid)))
    grad_gain = lax.optimization_barrier(jnp.sum(back_pre * first_conv, axis=(0, 1, 2, 3, 4)))
    grad_bias = lax.optimization_barrier(jnp.sum(back_pre, axis=(0, 1, 2, 3, 4)))
    back_conv = (back_pre * gain).astype(jnp.bfloat16)
    grad_one = grads_all(inputs, back_conv)
    grad_features = ((upstream.astype(jnp.float32) + conv_all(back_conv, flipped(weight_one))) * live_all).astype(jnp.bfloat16)
    scale = 1.0 / math.sqrt(devices * NB * VOX)
    return (out.reshape(SLABS_X, SLABS_Y, NB, width), grad_features.reshape(SLABS_X, SLABS_Y, NB, width), grad_one * scale, grad_two * scale, grad_gain * scale, grad_bias * scale)
```

```python
import functools
import math

import jax
import jax.numpy as jnp
from jax import lax
from jax.experimental import pallas as pl
from jax.experimental.pallas import tpu as pltpu
from jax.sharding import PartitionSpec as P

C = 96
LANES = 128
SIDE = 8
TAPS = 27
SPAN = TAPS * LANES
OWN = 512
RIM = 800
ROWS = 4096
F32 = jnp.float32
BF16 = jnp.bfloat16

VMEM_SPEC = pl.BlockSpec(memory_space=pltpu.VMEM)
SMEM_SPEC = pl.BlockSpec(memory_space=pltpu.SMEM)


def call(kernel, out_shape, specs, scratch=(), flops=0, moved=0, name=None, room=16):
    return pl.pallas_call(
        kernel,
        out_shape=out_shape,
        in_specs=specs,
        out_specs=jax.tree.map(lambda _: VMEM_SPEC, out_shape),
        scratch_shapes=list(scratch),
        cost_estimate=pl.CostEstimate(flops=flops, bytes_accessed=moved, transcendentals=0),
        name=name,
        compiler_params=pltpu.CompilerParams(vmem_limit_bytes=room << 20),
    )


def sublane_low(shape):
    return lax.broadcasted_iota(jnp.int32, shape, len(shape) - 2) < 4


def rotated(value, shift):
    flat = value.reshape((-1,) + value.shape[-2:])
    return pltpu.roll(flat, shift, 1).reshape(value.shape)


def grid_kernel(slots, features, cotangent, grid, low, high):
    count = features.shape[0]
    for field, source in enumerate((features, cotangent)):
        for i in range(2):
            for j in range(2):
                tiles, marks = [], []
                for k in range(2):
                    slot = slots[(i * 2 + j) * 2 + k]
                    filled = (slot < count).astype(F32)
                    brick = source[jnp.minimum(slot, count - 1)].astype(F32) * filled
                    tiles.append(brick.reshape(8, 8, C))
                    marks.append(filled)
                first, second = tiles
                is_low = sublane_low(first.shape)
                even = jnp.where(is_low, first, rotated(second, 4))
                odd = jnp.where(is_low, rotated(first, 4), second)
                joined = jnp.stack(
                    [even.reshape(4, 2, 8, C), odd.reshape(4, 2, 8, C)], axis=2
                ).reshape(4, 4, 8, C)
                at_x, at_y = slice(4 * i, 4 * i + 4), slice(4 * j, 4 * j + 4)
                grid[field, at_x, at_y, :, 0:C] = joined
                rest = (4, 4, 8, LANES - C)
                if field == 0:
                    mark = jnp.where(sublane_low(rest), marks[0], marks[1])
                else:
                    mark = jnp.zeros(rest, F32)
                grid[field, at_x, at_y, :, C:LANES] = mark
    for field in range(2):
        rows = slice(field * 128, field * 128 + 128)
        low[rows] = grid[field, 0:2].reshape(128, LANES).astype(BF16)
        high[rows] = grid[field, 6:8].reshape(128, LANES).astype(BF16)


def opened(message, lead):
    return message.astype(F32).reshape(lead + (SIDE, LANES))


def rim_kernel(grid, below, above, low, high):
    lower = opened(below[...], (2, 2, SIDE))
    upper = opened(above[...], (2, 2, SIDE))
    for message, at in ((low, 0), (high, SIDE - 2)):
        for field in range(2):
            base = field * 192
            message[base : base + 32] = (
                lower[field, :, at : at + 2].reshape(32, LANES).astype(BF16)
            )
            message[base + 32 : base + 160] = (
                grid[field, :, at : at + 2].reshape(128, LANES).astype(BF16)
            )
            message[base + 160 : base + 192] = (
                upper[field, :, at : at + 2].reshape(32, LANES).astype(BF16)
            )


def with_neighbours(value):
    spot = lax.broadcasted_iota(jnp.int32, value.shape, value.ndim - 2)
    before = jnp.where(spot == 0, 0.0, rotated(value, 1))
    after = jnp.where(spot == SIDE - 1, 0.0, rotated(value, SIDE - 1))
    return jnp.concatenate([before, value, after], axis=value.ndim - 1)


def fill_windows(windows, stacked, start, extent):
    rows = extent * extent * SIDE
    for wx in range(3):
        for wy in range(3):
            at = (wx * 3 + wy) * 3 * LANES
            piece = stacked[
                start + wx : start + wx + extent, start + wy : start + wy + extent
            ]
            windows[0:rows, at : at + 3 * LANES] = piece.reshape(rows, 3 * LANES).astype(BF16)


def spread(kernel, rows_ref):
    rows_ref[...] = jnp.zeros_like(rows_ref)
    for tap in range(TAPS):
        rows_ref[tap * LANES : tap * LANES + C, 0:C] = kernel[tap]


def spread_flipped(kernel, columns_ref):
    columns_ref[...] = jnp.zeros_like(columns_ref)
    for tap in range(TAPS):
        columns_ref[0:C, tap * LANES : tap * LANES + C] = kernel[TAPS - 1 - tap]


def plain_dot(left, right):
    return jnp.dot(left, right, preferred_element_type=F32)


def turned_dot(left, right):
    return lax.dot_general(left, right, (((1,), (1,)), ((), ())), preferred_element_type=F32)


def rounded(value):
    return value.astype(BF16).astype(F32)


def gradient_kernel(
    grid, below, above, left, right, weight_one, weight_two, gain_bias,
    result, inner,
    field_ref, stack_ref, windows, rows_ref, columns_ref, terms_one, terms_two, packed,
):
    lower = opened(below[...], (2, 2, SIDE))
    upper = opened(above[...], (2, 2, SIDE))
    to_left = opened(left[...], (2, SIDE + 4, 2))
    to_right = opened(right[...], (2, SIDE + 4, 2))

    def load_field(field):
        field_ref[2 : SIDE + 2, 2 : SIDE + 2] = grid[field]
        field_ref[0:2, 2 : SIDE + 2] = lower[field]
        field_ref[SIDE + 2 : SIDE + 4, 2 : SIDE + 2] = upper[field]
        field_ref[:, 0:2] = to_left[field]
        field_ref[:, SIDE + 2 : SIDE + 4] = to_right[field]

    gain, bias = gain_bias[0:1], gain_bias[1:2]
    spread(weight_one, rows_ref)
    spread_flipped(weight_two, columns_ref)
    load_field(0)
    mark = field_ref[1 : SIDE + 3, 1 : SIDE + 3].reshape(RIM, LANES)[:, C : C + 1]
    stack_ref[...] = with_neighbours(field_ref[...])
    fill_windows(windows, stack_ref, 0, SIDE + 2)
    first_conv = plain_dot(windows[...], rows_ref[...]) * mark
    pre = first_conv * gain + bias
    gate = 1.0 / (1.0 + jnp.exp(-pre))
    hidden = rounded(pre * gate * mark)
    slope = gate * (1.0 + pre * (1.0 - gate)) * mark
    inner[0:RIM] = hidden.astype(BF16)

    load_field(1)
    stack_ref[...] = with_neighbours(field_ref[...])
    fill_windows(windows, stack_ref, 0, SIDE + 2)
    back_hidden = turned_dot(windows[...], columns_ref[...])
    back_pre = back_hidden * slope
    back_conv = rounded(back_pre * gain)
    inner[RIM : 2 * RIM] = back_conv.astype(BF16)

    def own(value):
        lead = value.reshape(SIDE + 2, SIDE + 2, SIDE, LANES)
        return lead[1 : SIDE + 1, 1 : SIDE + 1].reshape(OWN, LANES)

    own_pre = own(back_pre)
    gain_term = jnp.sum(own_pre * own(first_conv), axis=0, keepdims=True)
    bias_term = jnp.sum(own_pre, axis=0, keepdims=True)

    fill_windows(windows, stack_ref, 1, SIDE)
    hidden_turned = own(hidden).T.astype(BF16)
    terms_two[...] = plain_dot(hidden_turned, windows[0:OWN])

    lead = back_conv.reshape(SIDE + 2, SIDE + 2, SIDE, LANES)
    stack_ref[0 : SIDE + 2, 0 : SIDE + 2] = with_neighbours(lead)
    fill_windows(windows, stack_ref, 0, SIDE)
    features_turned = grid[0].reshape(OWN, LANES).T.astype(BF16)
    terms_one[...] = plain_dot(features_turned, windows[0:OWN])

    def term(index):
        source = terms_one if index < TAPS else terms_two
        at = (TAPS - 1 - index % TAPS) * LANES
        return source[0:C, at : at + LANES]

    lane = lax.broadcasted_iota(jnp.int32, (C, LANES), 1)
    for group in range(13):
        split = term(4 * group + 3)
        for part in range(3):
            row = (3 * group + part) * C
            moved = pltpu.roll(split, C - 32 * part, 1)
            packed[row : row + C] = jnp.where(lane < C, term(4 * group + part), moved)
    packed[39 * C : 40 * C] = term(52)
    packed[40 * C : 41 * C] = term(53)
    packed[41 * C : ROWS] = jnp.zeros((ROWS - 41 * C, LANES), F32)
    packed[41 * C : 41 * C + 1] = gain_term
    packed[41 * C + 1 : 41 * C + 2] = bias_term
    result[...] = packed[...].astype(BF16)


def output_kernel(
    slots, grid, inner, weight_one, weight_two, out, grad,
    stack_ref, windows, rows_ref, columns_ref,
):
    count = out.shape[0]
    out[...] = jnp.zeros_like(out)
    grad[...] = jnp.zeros_like(grad)
    spread(weight_two, rows_ref)
    spread_flipped(weight_one, columns_ref)
    for field, target in enumerate((out, grad)):
        lead = inner[field * RIM : field * RIM + RIM].astype(F32)
        stack_ref[...] = with_neighbours(lead.reshape(SIDE + 2, SIDE + 2, SIDE, LANES))
        fill_windows(windows, stack_ref, 0, SIDE)
        if field == 0:
            total = plain_dot(windows[...], rows_ref[...])
        else:
            total = turned_dot(windows[...], columns_ref[...])
        dense = total.reshape(SIDE, SIDE, SIDE, LANES) + grid[field]
        for i in range(2):
            for j in range(2):
                column = dense[4 * i : 4 * i + 4, 4 * j : 4 * j + 4].reshape(4, 2, 2, 8, LANES)
                even = column[:, :, 0].reshape(8, 8, LANES)
                odd = column[:, :, 1].reshape(8, 8, LANES)
                is_low = sublane_low(even.shape)
                tiles = (
                    jnp.where(is_low, even, rotated(odd, 4)),
                    jnp.where(is_low, rotated(even, 4), odd),
                )
                for k in range(2):
                    slot = slots[(i * 2 + j) * 2 + k]
                    brick = tiles[k].reshape(64, LANES)[:, 0:C].astype(BF16)

                    @pl.when(slot < count)
                    def _():
                        target[slot] = brick


def finish_kernel(scale, total, grad_one, grad_two, grad_gain, grad_bias):
    lane = lax.broadcasted_iota(jnp.int32, (C, LANES), 1)

    def put(index, value):
        target = grad_one if index < TAPS else grad_two
        target[index % TAPS] = value[:, 0:C] * scale

    for group in range(13):
        parts = [total[(3 * group + part) * C : (3 * group + part + 1) * C] for part in range(3)]
        for part in range(3):
            put(4 * group + part, parts[part])
        moved = [pltpu.roll(parts[part], 32 * part + 32, 1) for part in range(3)]
        put(4 * group + 3, jnp.where(lane < 32, moved[0], jnp.where(lane < 64, moved[1], moved[2])))
    put(52, total[39 * C : 40 * C])
    put(53, total[40 * C : 41 * C])
    grad_gain[...] = total[41 * C : 41 * C + 1, 0:C] * scale
    grad_bias[...] = total[41 * C + 1 : 41 * C + 2, 0:C] * scale


def shape(dims, dtype):
    return jax.ShapeDtypeStruct(dims, dtype)


def dense_parts(features, cotangent, slots):
    return call(
        grid_kernel,
        (shape((2, SIDE, SIDE, SIDE, LANES), F32), shape((256, LANES), BF16), shape((256, LANES), BF16)),
        [SMEM_SPEC, VMEM_SPEC, VMEM_SPEC],
        moved=2_000_000,
        name="dense_grid",
    )(slots, features, cotangent)


def rims(grid, below, above):
    return call(
        rim_kernel,
        (shape((384, LANES), BF16), shape((384, LANES), BF16)),
        [VMEM_SPEC] * 3,
        moved=1_500_000,
        name="rims",
    )(grid, below, above)


def gradients(grid, halos, weight_one, weight_two, gain_bias):
    return call(
        gradient_kernel,
        (shape((ROWS, LANES), BF16), shape((2 * RIM, LANES), BF16)),
        [VMEM_SPEC] * 8,
        scratch=[
            pltpu.VMEM((SIDE + 4, SIDE + 4, SIDE, LANES), F32),
            pltpu.VMEM((SIDE + 4, SIDE + 4, SIDE, 3 * LANES), F32),
            pltpu.VMEM((RIM, SPAN), BF16),
            pltpu.VMEM((SPAN, LANES), BF16),
            pltpu.VMEM((LANES, SPAN), BF16),
            pltpu.VMEM((LANES, SPAN), F32),
            pltpu.VMEM((LANES, SPAN), F32),
            pltpu.VMEM((ROWS, LANES), F32),
        ],
        flops=2_400_000_000,
        moved=8_000_000,
        name="gradients",
        room=36,
    )(grid, *halos, weight_one, weight_two, gain_bias)


def outputs(slots, grid, inner, weight_one, weight_two):
    result = shape((4, 64, C), BF16)
    return call(
        output_kernel,
        (result, result),
        [SMEM_SPEC] + [VMEM_SPEC] * 4,
        scratch=[
            pltpu.VMEM((SIDE + 2, SIDE + 2, SIDE, 3 * LANES), F32),
            pltpu.VMEM((OWN, SPAN), BF16),
            pltpu.VMEM((SPAN, LANES), BF16),
            pltpu.VMEM((LANES, SPAN), BF16),
        ],
        flops=900_000_000,
        moved=4_000_000,
        name="outputs",
        room=24,
    )(slots, grid, inner, weight_one, weight_two)


def finish(total, scale):
    grads = shape((TAPS, C, C), F32)
    line = shape((1, C), F32)
    return call(
        functools.partial(finish_kernel, scale),
        (grads, grads, line, line),
        [VMEM_SPEC],
        moved=4_000_000,
        name="finish",
    )(total)


SIZES = dict(y=4, zh=4, core=2, zl=4, x=4)
PLANE = ("core", "y", "x")
LINE = ("zh", "zl")


def reduce_all(packed):
    plane, line = lax.axis_size(PLANE), lax.axis_size(LINE)
    rows = ROWS // plane
    parts = packed.reshape(plane, rows, LANES)
    parts = lax.all_to_all(parts, PLANE, 0, 0)
    chunk = jnp.sum(parts.astype(F32), axis=0)
    pieces = lax.all_to_all(chunk.reshape(line, rows // line, LANES), LINE, 0, 0)
    piece = jnp.sum(pieces, axis=0)
    chunk = lax.all_to_all(jnp.broadcast_to(piece, pieces.shape), LINE, 0, 0)
    chunk = chunk.reshape(rows, LANES)
    total = lax.all_to_all(jnp.broadcast_to(chunk, parts.shape), PLANE, 0, 0)
    return total.reshape(ROWS, LANES)


GX = ("y", "zh", "core")
GY = ("zl", "x")


def passed_along(block, axis, distance):
    devices = range(lax.axis_size(axis))
    route = [(i - distance, i) for i in devices if i - distance in devices]
    return lax.ppermute(block, axis, route)


def body(features, cotangent, brick_slot, weight_one, weight_two, gain, bias):
    slots = brick_slot.reshape(-1)
    source = features.reshape(4, 64, C)
    upstream = cotangent.reshape(4, 64, C)
    padded = jnp.pad(jnp.stack([gain, bias]), ((0, 0), (0, LANES - C)))
    grid, low, high = dense_parts(source, upstream, slots)
    below = passed_along(high, GX, 1)
    above = passed_along(low, GX, -1)
    low, high = rims(grid, below, above)
    left = passed_along(high, GY, 1)
    right = passed_along(low, GY, -1)
    packed, inner = gradients(grid, (below, above, left, right), weight_one, weight_two, padded)
    out, grad = outputs(slots, grid, inner, weight_one, weight_two)
    total = reduce_all(packed)
    scale = 1.0 / math.sqrt(lax.axis_size(GX) * lax.axis_size(GY) * 256)
    grad_one, grad_two, grad_gain, grad_bias = finish(total, scale)
    return (
        out.reshape(features.shape),
        grad.reshape(features.shape),
        grad_one,
        grad_two,
        grad_gain.reshape(gain.shape),
        grad_bias.reshape(bias.shape),
    )


def solution(mesh):
    fine = jax.sharding.Mesh(mesh.devices.reshape(tuple(SIZES.values())), tuple(SIZES))
    slabs = P(GX, GY, None, None)
    in_specs = (slabs, slabs, P(GX, GY, None, None, None), P(), P(), P(), P())
    out_specs = (slabs, slabs, P(), P(), P(), P())
    return jax.shard_map(body, mesh=fine, in_specs=in_specs, out_specs=out_specs, check_vma=False)
```

```python
import functools
import math

import jax
import jax.numpy as jnp
from jax import lax
from jax.experimental import pallas as pl
from jax.experimental.pallas import tpu as pltpu
from jax.sharding import PartitionSpec as P

C = 96
LANES = 128
SIDE = 8
TAPS = 27
SPAN = TAPS * LANES
OWN = 512
RIM = 800
ROWS = 4096
F32 = jnp.float32
BF16 = jnp.bfloat16

VMEM_SPEC = pl.BlockSpec(memory_space=pltpu.VMEM)
SMEM_SPEC = pl.BlockSpec(memory_space=pltpu.SMEM)


def call(kernel, out_shape, specs, scratch=(), flops=0, moved=0, name=None, room=16):
    return pl.pallas_call(
        kernel,
        out_shape=out_shape,
        in_specs=specs,
        out_specs=jax.tree.map(lambda _: VMEM_SPEC, out_shape),
        scratch_shapes=list(scratch),
        cost_estimate=pl.CostEstimate(flops=flops, bytes_accessed=moved, transcendentals=0),
        name=name,
        compiler_params=pltpu.CompilerParams(vmem_limit_bytes=room << 20),
    )


def sublane_low(shape):
    return lax.broadcasted_iota(jnp.int32, shape, len(shape) - 2) < 4


def rotated(value, shift):
    flat = value.reshape((-1,) + value.shape[-2:])
    return pltpu.roll(flat, shift, 1).reshape(value.shape)


def grid_kernel(slots, features, cotangent, grid, low, high):
    count = features.shape[0]
    for field, source in enumerate((features, cotangent)):
        for i in range(2):
            for j in range(2):
                tiles, marks = [], []
                for k in range(2):
                    slot = slots[0, 0, i, j, k]
                    filled = (slot < count).astype(F32)
                    brick = source[jnp.minimum(slot, count - 1)].astype(F32) * filled
                    tiles.append(brick.reshape(8, 8, C))
                    marks.append(filled)
                first, second = tiles
                is_low = sublane_low(first.shape)
                even = jnp.where(is_low, first, rotated(second, 4))
                odd = jnp.where(is_low, rotated(first, 4), second)
                joined = jnp.stack(
                    [even.reshape(4, 2, 8, C), odd.reshape(4, 2, 8, C)], axis=2
                ).reshape(4, 4, 8, C)
                at_x, at_y = slice(4 * i, 4 * i + 4), slice(4 * j, 4 * j + 4)
                grid[field, at_x, at_y, :, 0:C] = joined
                rest = (4, 4, 8, LANES - C)
                if field == 0:
                    mark = jnp.where(sublane_low(rest), marks[0], marks[1])
                else:
                    mark = jnp.zeros(rest, F32)
                grid[field, at_x, at_y, :, C:LANES] = mark
    for field in range(2):
        rows = slice(field * 128, field * 128 + 128)
        low[rows] = grid[field, 0:2].reshape(128, LANES).astype(BF16)
        high[rows] = grid[field, 6:8].reshape(128, LANES).astype(BF16)


def opened(message, lead):
    return message.astype(F32).reshape(lead + (SIDE, LANES))


def rim_kernel(grid, below, above, low, high):
    lower = opened(below[...], (2, 2, SIDE))
    upper = opened(above[...], (2, 2, SIDE))
    for message, at in ((low, 0), (high, SIDE - 2)):
        for field in range(2):
            base = field * 192
            message[base : base + 32] = (
                lower[field, :, at : at + 2].reshape(32, LANES).astype(BF16)
            )
            message[base + 32 : base + 160] = (
                grid[field, :, at : at + 2].reshape(128, LANES).astype(BF16)
            )
            message[base + 160 : base + 192] = (
                upper[field, :, at : at + 2].reshape(32, LANES).astype(BF16)
            )


def with_neighbours(value):
    spot = lax.broadcasted_iota(jnp.int32, value.shape, value.ndim - 2)
    before = jnp.where(spot == 0, 0.0, rotated(value, 1))
    after = jnp.where(spot == SIDE - 1, 0.0, rotated(value, SIDE - 1))
    return jnp.concatenate([before, value, after], axis=value.ndim - 1)


def fill_windows(windows, stacked, start, extent):
    rows = extent * extent * SIDE
    for wx in range(3):
        for wy in range(3):
            at = (wx * 3 + wy) * 3 * LANES
            piece = stacked[
                start + wx : start + wx + extent, start + wy : start + wy + extent
            ]
            windows[0:rows, at : at + 3 * LANES] = piece.reshape(rows, 3 * LANES).astype(BF16)


def spread(kernel, rows_ref):
    rows_ref[...] = jnp.zeros_like(rows_ref)
    for tap in range(TAPS):
        rows_ref[tap * LANES : tap * LANES + C, 0:C] = kernel[tap]


def spread_flipped(kernel, columns_ref):
    columns_ref[...] = jnp.zeros_like(columns_ref)
    for tap in range(TAPS):
        columns_ref[0:C, tap * LANES : tap * LANES + C] = kernel[TAPS - 1 - tap]


def prepare_kernel(
    weight_one, weight_two, gain, bias, rows_one, columns_two, rows_two, columns_one, gain_bias
):
    spread(weight_one, rows_one)
    spread(weight_two, rows_two)
    spread_flipped(weight_one, columns_one)
    spread_flipped(weight_two, columns_two)
    gain_bias[...] = jnp.zeros_like(gain_bias)
    gain_bias[0:1, 0:C] = gain[...]
    gain_bias[1:2, 0:C] = bias[...]


def plain_dot(left, right):
    return jnp.dot(left, right, preferred_element_type=F32)


def turned_dot(left, right):
    return lax.dot_general(left, right, (((1,), (1,)), ((), ())), preferred_element_type=F32)


def rounded(value):
    return value.astype(BF16).astype(F32)


def gradient_kernel(
    grid, below, above, left, right, rows_ref, columns_ref, gain_bias,
    result, inner,
    field_ref, stack_ref, windows, terms_one, terms_two, packed,
):
    lower = opened(below[...], (2, 2, SIDE))
    upper = opened(above[...], (2, 2, SIDE))
    to_left = opened(left[...], (2, SIDE + 4, 2))
    to_right = opened(right[...], (2, SIDE + 4, 2))

    def load_field(field):
        field_ref[2 : SIDE + 2, 2 : SIDE + 2] = grid[field]
        field_ref[0:2, 2 : SIDE + 2] = lower[field]
        field_ref[SIDE + 2 : SIDE + 4, 2 : SIDE + 2] = upper[field]
        field_ref[:, 0:2] = to_left[field]
        field_ref[:, SIDE + 2 : SIDE + 4] = to_right[field]

    gain, bias = gain_bias[0:1], gain_bias[1:2]
    load_field(0)
    mark = field_ref[1 : SIDE + 3, 1 : SIDE + 3].reshape(RIM, LANES)[:, C : C + 1]
    stack_ref[...] = with_neighbours(field_ref[...])
    fill_windows(windows, stack_ref, 0, SIDE + 2)
    first_conv = plain_dot(windows[...], rows_ref[...]) * mark
    pre = first_conv * gain + bias
    gate = 1.0 / (1.0 + jnp.exp(-pre))
    hidden = rounded(pre * gate * mark)
    slope = gate * (1.0 + pre * (1.0 - gate)) * mark
    inner[0:RIM] = hidden.astype(BF16)

    load_field(1)
    stack_ref[...] = with_neighbours(field_ref[...])
    fill_windows(windows, stack_ref, 0, SIDE + 2)
    back_hidden = turned_dot(windows[...], columns_ref[...])
    back_pre = back_hidden * slope
    back_conv = rounded(back_pre * gain)
    inner[RIM : 2 * RIM] = back_conv.astype(BF16)

    def own(value):
        lead = value.reshape(SIDE + 2, SIDE + 2, SIDE, LANES)
        return lead[1 : SIDE + 1, 1 : SIDE + 1].reshape(OWN, LANES)

    own_pre = own(back_pre)
    gain_term = jnp.sum(own_pre * own(first_conv), axis=0, keepdims=True)
    bias_term = jnp.sum(own_pre, axis=0, keepdims=True)

    fill_windows(windows, stack_ref, 1, SIDE)
    hidden_turned = own(hidden).T.astype(BF16)
    terms_two[...] = plain_dot(hidden_turned, windows[0:OWN])

    lead = back_conv.reshape(SIDE + 2, SIDE + 2, SIDE, LANES)
    stack_ref[0 : SIDE + 2, 0 : SIDE + 2] = with_neighbours(lead)
    fill_windows(windows, stack_ref, 0, SIDE)
    features_turned = grid[0].reshape(OWN, LANES).T.astype(BF16)
    terms_one[...] = plain_dot(features_turned, windows[0:OWN])

    def term(index):
        source = terms_one if index < TAPS else terms_two
        at = (TAPS - 1 - index % TAPS) * LANES
        return source[0:C, at : at + LANES]

    lane = lax.broadcasted_iota(jnp.int32, (C, LANES), 1)
    for group in range(13):
        split = term(4 * group + 3)
        for part in range(3):
            row = (3 * group + part) * C
            moved = pltpu.roll(split, C - 32 * part, 1)
            packed[row : row + C] = jnp.where(lane < C, term(4 * group + part), moved)
    packed[39 * C : 40 * C] = term(52)
    packed[40 * C : 41 * C] = term(53)
    packed[41 * C : ROWS] = jnp.zeros((ROWS - 41 * C, LANES), F32)
    for spot, value in enumerate((gain_term, bias_term)):
        base = 41 * C + 2 * spot
        packed[base : base + 1] = rounded(value)
        packed[base + 1 : base + 2] = value - rounded(value)
    result[...] = packed[...].astype(BF16)


def output_kernel(
    slots, grid, inner, rows_ref, columns_ref, out, grad,
    stack_ref, windows,
):
    count = out.shape[0]
    out[...] = jnp.zeros_like(out)
    grad[...] = jnp.zeros_like(grad)
    for field, target in enumerate((out, grad)):
        lead = inner[field * RIM : field * RIM + RIM].astype(F32)
        stack_ref[...] = with_neighbours(lead.reshape(SIDE + 2, SIDE + 2, SIDE, LANES))
        fill_windows(windows, stack_ref, 0, SIDE)
        if field == 0:
            total = plain_dot(windows[...], rows_ref[...])
        else:
            total = turned_dot(windows[...], columns_ref[...])
        dense = total.reshape(SIDE, SIDE, SIDE, LANES) + grid[field]
        for i in range(2):
            for j in range(2):
                column = dense[4 * i : 4 * i + 4, 4 * j : 4 * j + 4].reshape(4, 2, 2, 8, LANES)
                even = column[:, :, 0].reshape(8, 8, LANES)
                odd = column[:, :, 1].reshape(8, 8, LANES)
                is_low = sublane_low(even.shape)
                tiles = (
                    jnp.where(is_low, even, rotated(odd, 4)),
                    jnp.where(is_low, rotated(even, 4), odd),
                )
                for k in range(2):
                    slot = slots[0, 0, i, j, k]
                    brick = tiles[k].reshape(64, LANES)[:, 0:C].astype(BF16)

                    @pl.when(slot < count)
                    def _():
                        target[slot] = brick


def finish_kernel(scale, side, mine, other, grad_one, grad_two, grad_gain, grad_bias, total):
    half = ROWS // 2
    at = pl.multiple_of(side[0] * half, half)
    total[pl.ds(at, half)] = mine[...]
    total[pl.ds(half - at, half)] = other[...]
    lane = lax.broadcasted_iota(jnp.int32, (C, LANES), 1)

    def put(index, value):
        target = grad_one if index < TAPS else grad_two
        target[index % TAPS] = value[:, 0:C] * scale

    for group in range(13):
        parts = [total[(3 * group + part) * C : (3 * group + part + 1) * C] for part in range(3)]
        for part in range(3):
            put(4 * group + part, parts[part])
        moved = [pltpu.roll(parts[part], 32 * part + 32, 1) for part in range(3)]
        put(4 * group + 3, jnp.where(lane < 32, moved[0], jnp.where(lane < 64, moved[1], moved[2])))
    put(52, total[39 * C : 40 * C])
    put(53, total[40 * C : 41 * C])
    for spot, target in enumerate((grad_gain, grad_bias)):
        base = 41 * C + 2 * spot
        target[...] = (total[base : base + 1, 0:C] + total[base + 1 : base + 2, 0:C]) * scale


def shape(dims, dtype):
    return jax.ShapeDtypeStruct(dims, dtype)


def dense_parts(features, cotangent, slots):
    return call(
        grid_kernel,
        (shape((2, SIDE, SIDE, SIDE, LANES), F32), shape((256, LANES), BF16), shape((256, LANES), BF16)),
        [SMEM_SPEC, VMEM_SPEC, VMEM_SPEC],
        moved=2_000_000,
        name="dense_grid",
    )(slots, features, cotangent)


def rims(grid, below, above):
    return call(
        rim_kernel,
        (shape((384, LANES), BF16), shape((384, LANES), BF16)),
        [VMEM_SPEC] * 3,
        moved=1_500_000,
        name="rims",
    )(grid, below, above)


def gradients(grid, halos, rows, columns, gain_bias):
    return call(
        gradient_kernel,
        (shape((ROWS, LANES), BF16), shape((2 * RIM, LANES), BF16)),
        [VMEM_SPEC] * 8,
        scratch=[
            pltpu.VMEM((SIDE + 4, SIDE + 4, SIDE, LANES), F32),
            pltpu.VMEM((SIDE + 4, SIDE + 4, SIDE, 3 * LANES), F32),
            pltpu.VMEM((RIM, SPAN), BF16),
            pltpu.VMEM((LANES, SPAN), F32),
            pltpu.VMEM((LANES, SPAN), F32),
            pltpu.VMEM((ROWS, LANES), F32),
        ],
        flops=2_400_000_000,
        moved=8_000_000,
        name="gradients",
        room=36,
    )(grid, *halos, rows, columns, gain_bias)


def outputs(slots, grid, inner, rows, columns):
    result = shape((4, 64, C), BF16)
    return call(
        output_kernel,
        (result, result),
        [SMEM_SPEC] + [VMEM_SPEC] * 4,
        scratch=[
            pltpu.VMEM((SIDE + 2, SIDE + 2, SIDE, 3 * LANES), F32),
            pltpu.VMEM((OWN, SPAN), BF16),
        ],
        flops=900_000_000,
        moved=4_000_000,
        name="outputs",
        room=24,
    )(slots, grid, inner, rows, columns)


def finish(side, mine, other, scale):
    grads = shape((TAPS, C, C), F32)
    line = shape((1, C), F32)
    return call(
        functools.partial(finish_kernel, scale),
        (grads, grads, line, line),
        [SMEM_SPEC, VMEM_SPEC, VMEM_SPEC],
        scratch=[pltpu.VMEM((ROWS, LANES), F32)],
        moved=4_000_000,
        name="finish",
    )(side, mine, other)


def prepare(weight_one, weight_two, gain, bias):
    rows, columns = shape((SPAN, LANES), BF16), shape((LANES, SPAN), BF16)
    return call(
        prepare_kernel,
        (rows, columns, rows, columns, shape((2, LANES), F32)),
        [VMEM_SPEC] * 4,
        moved=6_000_000,
        name="prepare",
    )(weight_one, weight_two, gain.reshape(1, C), bias.reshape(1, C))


SIZES = dict(y=4, zh=4, core=2, zl=2, zp=2, x=4)
PLANE = ("y", "x", "zp")
LINE = ("zh", "zl")


def spread_out(block, axes):
    copies = jnp.broadcast_to(block, (lax.axis_size(axes),) + block.shape)
    return lax.all_to_all(copies, axes, 0, 0)


def reduce_all(packed):
    group = ("core",) + PLANE
    rows = ROWS // lax.axis_size(group)
    parts = lax.all_to_all(packed.reshape(-1, rows, LANES), group, 0, 0)
    chunk = jnp.sum(parts.astype(F32), axis=0)
    chunk = jnp.sum(spread_out(chunk, LINE), axis=0)
    return spread_out(chunk, PLANE).reshape(ROWS // 2, LANES)


GX = ("y", "zh", "core")
GY = ("zl", "zp", "x")


def passed_along(block, axis, distance):
    devices = range(lax.axis_size(axis))
    route = [(i - distance, i) for i in devices if i - distance in devices]
    return lax.ppermute(block, axis, route)


def body(features, cotangent, brick_slot, weight_one, weight_two, gain, bias):
    source = features.reshape(4, 64, C)
    upstream = cotangent.reshape(4, 64, C)
    rows_one, columns_two, rows_two, columns_one, gain_bias = prepare(weight_one, weight_two, gain, bias)
    grid, low, high = dense_parts(source, upstream, brick_slot)
    below = passed_along(high, GX, 1)
    above = passed_along(low, GX, -1)
    low, high = rims(grid, below, above)
    left = passed_along(high, GY, 1)
    right = passed_along(low, GY, -1)
    packed, inner = gradients(grid, (below, above, left, right), rows_one, columns_two, gain_bias)
    out, grad = outputs(brick_slot, grid, inner, rows_two, columns_one)
    out, grad = out.reshape(features.shape), grad.reshape(features.shape)
    mine, out, grad = lax.optimization_barrier((reduce_all(packed), out, grad))
    other = lax.ppermute(mine, "core", [(0, 1), (1, 0)])
    scale = 1.0 / math.sqrt(lax.axis_size(GX) * lax.axis_size(GY) * 256)
    grad_one, grad_two, grad_gain, grad_bias = finish(lax.axis_index("core").reshape(1), mine, other, scale)
    return (
        out,
        grad,
        grad_one,
        grad_two,
        grad_gain.reshape(gain.shape),
        grad_bias.reshape(bias.shape),
    )


def solution(mesh):
    fine = jax.sharding.Mesh(mesh.devices.reshape(tuple(SIZES.values())), tuple(SIZES))
    slabs = P(GX, GY, None, None)
    in_specs = (slabs, slabs, P(GX, GY, None, None, None), P(), P(), P(), P())
    out_specs = (slabs, slabs, P(), P(), P(), P())
    return jax.shard_map(body, mesh=fine, in_specs=in_specs, out_specs=out_specs, check_vma=False)
```

```python
import functools
import math

import jax
import jax.numpy as jnp
from jax import lax
from jax.experimental import pallas as pl
from jax.experimental.pallas import tpu as pltpu
from jax.sharding import PartitionSpec as P

C = 96
LANES = 128
SIDE = 8
TAPS = 27
SPAN = TAPS * LANES
OWN = 512
RIM = 800
ROWS = 4096
F32 = jnp.float32
BF16 = jnp.bfloat16

VMEM_SPEC = pl.BlockSpec(memory_space=pltpu.VMEM)
SMEM_SPEC = pl.BlockSpec(memory_space=pltpu.SMEM)


def call(kernel, out_shape, specs, scratch=(), flops=0, moved=0, name=None, room=16):
    return pl.pallas_call(
        kernel,
        out_shape=out_shape,
        in_specs=specs,
        out_specs=jax.tree.map(lambda _: VMEM_SPEC, out_shape),
        scratch_shapes=list(scratch),
        cost_estimate=pl.CostEstimate(flops=flops, bytes_accessed=moved, transcendentals=0),
        name=name,
        compiler_params=pltpu.CompilerParams(vmem_limit_bytes=room << 20),
    )


def sublane_low(shape):
    return lax.broadcasted_iota(jnp.int32, shape, len(shape) - 2) < 4


def rotated(value, shift):
    flat = value.reshape((-1,) + value.shape[-2:])
    return pltpu.roll(flat, shift, 1).reshape(value.shape)


def grid_kernel(slots, features, cotangent, grid, low, high):
    count = features.shape[0]
    for field, source in enumerate((features, cotangent)):
        for i in range(2):
            for j in range(2):
                tiles, marks = [], []
                for k in range(2):
                    slot = slots[0, 0, i, j, k]
                    filled = (slot < count).astype(F32)
                    brick = source[jnp.minimum(slot, count - 1)].astype(F32) * filled
                    tiles.append(brick.reshape(8, 8, C))
                    marks.append(filled)
                first, second = tiles
                is_low = sublane_low(first.shape)
                even = jnp.where(is_low, first, rotated(second, 4))
                odd = jnp.where(is_low, rotated(first, 4), second)
                joined = jnp.stack(
                    [even.reshape(4, 2, 8, C), odd.reshape(4, 2, 8, C)], axis=2
                ).reshape(4, 4, 8, C)
                at_x, at_y = slice(4 * i, 4 * i + 4), slice(4 * j, 4 * j + 4)
                grid[field, at_x, at_y, :, 0:C] = joined
                rest = (4, 4, 8, LANES - C)
                if field == 0:
                    mark = jnp.where(sublane_low(rest), marks[0], marks[1])
                else:
                    mark = jnp.zeros(rest, F32)
                grid[field, at_x, at_y, :, C:LANES] = mark
    for field in range(2):
        rows = slice(field * 128, field * 128 + 128)
        low[rows] = grid[field, 0:2].reshape(128, LANES).astype(BF16)
        high[rows] = grid[field, 6:8].reshape(128, LANES).astype(BF16)


def opened(message, lead):
    return message.astype(F32).reshape(lead + (SIDE, LANES))


def rim_kernel(grid, below, above, low, high):
    lower = opened(below[...], (2, 2, SIDE))
    upper = opened(above[...], (2, 2, SIDE))
    for message, at in ((low, 0), (high, SIDE - 2)):
        for field in range(2):
            base = field * 192
            message[base : base + 32] = (
                lower[field, :, at : at + 2].reshape(32, LANES).astype(BF16)
            )
            message[base + 32 : base + 160] = (
                grid[field, :, at : at + 2].reshape(128, LANES).astype(BF16)
            )
            message[base + 160 : base + 192] = (
                upper[field, :, at : at + 2].reshape(32, LANES).astype(BF16)
            )


def with_neighbours(value):
    spot = lax.broadcasted_iota(jnp.int32, value.shape, value.ndim - 2)
    before = jnp.where(spot == 0, 0.0, rotated(value, 1))
    after = jnp.where(spot == SIDE - 1, 0.0, rotated(value, SIDE - 1))
    return jnp.concatenate([before, value, after], axis=value.ndim - 1)


def fill_windows(windows, stacked, start, extent):
    rows = extent * extent * SIDE
    for wx in range(3):
        for wy in range(3):
            at = (wx * 3 + wy) * 3 * LANES
            piece = stacked[
                start + wx : start + wx + extent, start + wy : start + wy + extent
            ]
            windows[0:rows, at : at + 3 * LANES] = piece.reshape(rows, 3 * LANES).astype(BF16)


def spread(kernel, rows_ref):
    rows_ref[...] = jnp.zeros_like(rows_ref)
    for tap in range(TAPS):
        rows_ref[tap * LANES : tap * LANES + C, 0:C] = kernel[tap]


def spread_flipped(kernel, columns_ref):
    columns_ref[...] = jnp.zeros_like(columns_ref)
    for tap in range(TAPS):
        columns_ref[0:C, tap * LANES : tap * LANES + C] = kernel[TAPS - 1 - tap]


def prepare_kernel(
    weight_one, weight_two, gain, bias, rows_one, columns_two, rows_two, columns_one, gain_bias
):
    spread(weight_one, rows_one)
    spread(weight_two, rows_two)
    spread_flipped(weight_one, columns_one)
    spread_flipped(weight_two, columns_two)
    gain_bias[...] = jnp.zeros_like(gain_bias)
    gain_bias[0:1, 0:C] = gain[...]
    gain_bias[1:2, 0:C] = bias[...]


def plain_dot(left, right):
    return jnp.dot(left, right, preferred_element_type=F32)


def turned_dot(left, right):
    return lax.dot_general(left, right, (((1,), (1,)), ((), ())), preferred_element_type=F32)


def rounded(value):
    return value.astype(BF16).astype(F32)


def gradient_kernel(
    grid, below, above, left, right, rows_ref, columns_ref, gain_bias,
    result, inner,
    field_ref, stack_ref, windows, terms_one, terms_two, packed,
):
    lower = opened(below[...], (2, 2, SIDE))
    upper = opened(above[...], (2, 2, SIDE))
    to_left = opened(left[...], (2, SIDE + 4, 2))
    to_right = opened(right[...], (2, SIDE + 4, 2))

    def load_field(field):
        field_ref[2 : SIDE + 2, 2 : SIDE + 2] = grid[field]
        field_ref[0:2, 2 : SIDE + 2] = lower[field]
        field_ref[SIDE + 2 : SIDE + 4, 2 : SIDE + 2] = upper[field]
        field_ref[:, 0:2] = to_left[field]
        field_ref[:, SIDE + 2 : SIDE + 4] = to_right[field]

    gain, bias = gain_bias[0:1], gain_bias[1:2]
    load_field(0)
    mark = field_ref[1 : SIDE + 3, 1 : SIDE + 3].reshape(RIM, LANES)[:, C : C + 1]
    stack_ref[...] = with_neighbours(field_ref[...])
    fill_windows(windows, stack_ref, 0, SIDE + 2)
    first_conv = plain_dot(windows[...], rows_ref[...]) * mark
    pre = first_conv * gain + bias
    gate = 1.0 / (1.0 + jnp.exp(-pre))
    hidden = rounded(pre * gate * mark)
    slope = gate * (1.0 + pre * (1.0 - gate)) * mark
    inner[0:RIM] = hidden.astype(BF16)

    load_field(1)
    stack_ref[...] = with_neighbours(field_ref[...])
    fill_windows(windows, stack_ref, 0, SIDE + 2)
    back_hidden = turned_dot(windows[...], columns_ref[...])
    back_pre = back_hidden * slope
    back_conv = rounded(back_pre * gain)
    inner[RIM : 2 * RIM] = back_conv.astype(BF16)

    def own(value):
        lead = value.reshape(SIDE + 2, SIDE + 2, SIDE, LANES)
        return lead[1 : SIDE + 1, 1 : SIDE + 1].reshape(OWN, LANES)

    own_pre = own(back_pre)
    gain_term = jnp.sum(own_pre * own(first_conv), axis=0, keepdims=True)
    bias_term = jnp.sum(own_pre, axis=0, keepdims=True)

    fill_windows(windows, stack_ref, 1, SIDE)
    hidden_turned = own(hidden).T.astype(BF16)
    terms_two[...] = plain_dot(hidden_turned, windows[0:OWN])

    lead = back_conv.reshape(SIDE + 2, SIDE + 2, SIDE, LANES)
    stack_ref[0 : SIDE + 2, 0 : SIDE + 2] = with_neighbours(lead)
    fill_windows(windows, stack_ref, 0, SIDE)
    features_turned = grid[0].reshape(OWN, LANES).T.astype(BF16)
    terms_one[...] = plain_dot(features_turned, windows[0:OWN])

    def term(index):
        source = terms_one if index < TAPS else terms_two
        at = (TAPS - 1 - index % TAPS) * LANES
        return source[0:C, at : at + LANES]

    lane = lax.broadcasted_iota(jnp.int32, (C, LANES), 1)
    for group in range(13):
        split = term(4 * group + 3)
        for part in range(3):
            row = (3 * group + part) * C
            moved = pltpu.roll(split, C - 32 * part, 1)
            packed[row : row + C] = jnp.where(lane < C, term(4 * group + part), moved)
    packed[39 * C : 40 * C] = term(52)
    packed[40 * C : 41 * C] = term(53)
    packed[41 * C : ROWS] = jnp.zeros((ROWS - 41 * C, LANES), F32)
    for spot, value in enumerate((gain_term, bias_term)):
        base = 41 * C + 2 * spot
        packed[base : base + 1] = rounded(value)
        packed[base + 1 : base + 2] = value - rounded(value)
    result[...] = packed[...].astype(BF16)


def output_kernel(
    slots, grid, inner, rows_ref, columns_ref, out, grad,
    stack_ref, windows,
):
    count = out.shape[0]
    out[...] = jnp.zeros_like(out)
    grad[...] = jnp.zeros_like(grad)
    for field, target in enumerate((out, grad)):
        lead = inner[field * RIM : field * RIM + RIM].astype(F32)
        stack_ref[...] = with_neighbours(lead.reshape(SIDE + 2, SIDE + 2, SIDE, LANES))
        fill_windows(windows, stack_ref, 0, SIDE)
        if field == 0:
            total = plain_dot(windows[...], rows_ref[...])
        else:
            total = turned_dot(windows[...], columns_ref[...])
        dense = total.reshape(SIDE, SIDE, SIDE, LANES) + grid[field]
        for i in range(2):
            for j in range(2):
                column = dense[4 * i : 4 * i + 4, 4 * j : 4 * j + 4].reshape(4, 2, 2, 8, LANES)
                even = column[:, :, 0].reshape(8, 8, LANES)
                odd = column[:, :, 1].reshape(8, 8, LANES)
                is_low = sublane_low(even.shape)
                tiles = (
                    jnp.where(is_low, even, rotated(odd, 4)),
                    jnp.where(is_low, rotated(even, 4), odd),
                )
                for k in range(2):
                    slot = slots[0, 0, i, j, k]
                    brick = tiles[k].reshape(64, LANES)[:, 0:C].astype(BF16)

                    @pl.when(slot < count)
                    def _():
                        target[slot] = brick


def finish_kernel(scale, parts, grad_one, grad_two, grad_gain, grad_bias, total):
    total[...] = parts[...].astype(F32)
    lane = lax.broadcasted_iota(jnp.int32, (C, LANES), 1)

    def put(index, value):
        target = grad_one if index < TAPS else grad_two
        target[index % TAPS] = value[:, 0:C] * scale

    for group in range(13):
        parts = [total[(3 * group + part) * C : (3 * group + part + 1) * C] for part in range(3)]
        for part in range(3):
            put(4 * group + part, parts[part])
        moved = [pltpu.roll(parts[part], 32 * part + 32, 1) for part in range(3)]
        put(4 * group + 3, jnp.where(lane < 32, moved[0], jnp.where(lane < 64, moved[1], moved[2])))
    put(52, total[39 * C : 40 * C])
    put(53, total[40 * C : 41 * C])
    for spot, target in enumerate((grad_gain, grad_bias)):
        base = 41 * C + 2 * spot
        target[...] = (total[base : base + 1, 0:C] + total[base + 1 : base + 2, 0:C]) * scale


def shape(dims, dtype):
    return jax.ShapeDtypeStruct(dims, dtype)


def dense_parts(features, cotangent, slots):
    return call(
        grid_kernel,
        (shape((2, SIDE, SIDE, SIDE, LANES), F32), shape((256, LANES), BF16), shape((256, LANES), BF16)),
        [SMEM_SPEC, VMEM_SPEC, VMEM_SPEC],
        moved=2_000_000,
        name="dense_grid",
    )(slots, features, cotangent)


def rims(grid, below, above):
    return call(
        rim_kernel,
        (shape((384, LANES), BF16), shape((384, LANES), BF16)),
        [VMEM_SPEC] * 3,
        moved=1_500_000,
        name="rims",
    )(grid, below, above)


def gradients(grid, halos, rows, columns, gain_bias):
    return call(
        gradient_kernel,
        (shape((ROWS, LANES), BF16), shape((2 * RIM, LANES), BF16)),
        [VMEM_SPEC] * 8,
        scratch=[
            pltpu.VMEM((SIDE + 4, SIDE + 4, SIDE, LANES), F32),
            pltpu.VMEM((SIDE + 4, SIDE + 4, SIDE, 3 * LANES), F32),
            pltpu.VMEM((RIM, SPAN), BF16),
            pltpu.VMEM((LANES, SPAN), F32),
            pltpu.VMEM((LANES, SPAN), F32),
            pltpu.VMEM((ROWS, LANES), F32),
        ],
        flops=2_400_000_000,
        moved=8_000_000,
        name="gradients",
        room=36,
    )(grid, *halos, rows, columns, gain_bias)


def outputs(slots, grid, inner, rows, columns):
    result = shape((4, 64, C), BF16)
    return call(
        output_kernel,
        (result, result),
        [SMEM_SPEC] + [VMEM_SPEC] * 4,
        scratch=[
            pltpu.VMEM((SIDE + 2, SIDE + 2, SIDE, 3 * LANES), F32),
            pltpu.VMEM((OWN, SPAN), BF16),
        ],
        flops=900_000_000,
        moved=4_000_000,
        name="outputs",
        room=24,
    )(slots, grid, inner, rows, columns)


def finish(total, scale):
    grads = shape((TAPS, C, C), F32)
    line = shape((1, C), F32)
    return call(
        functools.partial(finish_kernel, scale),
        (grads, grads, line, line),
        [VMEM_SPEC],
        scratch=[pltpu.VMEM((ROWS, LANES), F32)],
        moved=4_000_000,
        name="finish",
    )(total)


def prepare(weight_one, weight_two, gain, bias):
    rows, columns = shape((SPAN, LANES), BF16), shape((LANES, SPAN), BF16)
    return call(
        prepare_kernel,
        (rows, columns, rows, columns, shape((2, LANES), F32)),
        [VMEM_SPEC] * 4,
        moved=6_000_000,
        name="prepare",
    )(weight_one, weight_two, gain.reshape(1, C), bias.reshape(1, C))


SIZES = dict(y=4, zh=4, core=2, zl=2, zp=2, x=4)
PLANE = ("core", "y", "x", "zp")
LINE = ("zh", "zl")


def spread_out(block, axes):
    copies = jnp.broadcast_to(block, (lax.axis_size(axes),) + block.shape)
    return lax.all_to_all(copies, axes, 0, 0)


def reduce_all(packed):
    rows = ROWS // lax.axis_size(PLANE)
    parts = lax.all_to_all(packed.reshape(-1, rows, LANES), PLANE, 0, 0)
    chunk = jnp.sum(parts.astype(F32), axis=0)
    chunk = jnp.sum(spread_out(chunk, LINE), axis=0)
    return spread_out(chunk.astype(BF16), PLANE).reshape(ROWS, LANES)


GX = ("y", "zh", "core")
GY = ("zl", "zp", "x")


def passed_along(block, axis, distance):
    devices = range(lax.axis_size(axis))
    route = [(i - distance, i) for i in devices if i - distance in devices]
    return lax.ppermute(block, axis, route)


def body(features, cotangent, brick_slot, weight_one, weight_two, gain, bias):
    source = features.reshape(4, 64, C)
    upstream = cotangent.reshape(4, 64, C)
    grid, low, high = dense_parts(source, upstream, brick_slot)
    low, high, *parameters = lax.optimization_barrier((low, high, weight_one, weight_two, gain, bias))
    below = passed_along(high, GX, 1)
    above = passed_along(low, GX, -1)
    prepared = prepare(*parameters)
    below, above, prepared = lax.optimization_barrier((below, above, prepared))
    rows_one, columns_two, rows_two, columns_one, gain_bias = prepared
    low, high = rims(grid, below, above)
    left = passed_along(high, GY, 1)
    right = passed_along(low, GY, -1)
    packed, inner = gradients(grid, (below, above, left, right), rows_one, columns_two, gain_bias)
    out, grad = outputs(brick_slot, grid, inner, rows_two, columns_one)
    out, grad = out.reshape(features.shape), grad.reshape(features.shape)
    total = reduce_all(packed)
    scale = 1.0 / math.sqrt(lax.axis_size(GX) * lax.axis_size(GY) * 256)
    grad_one, grad_two, grad_gain, grad_bias = finish(total, scale)
    return (
        out,
        grad,
        grad_one,
        grad_two,
        grad_gain.reshape(gain.shape),
        grad_bias.reshape(bias.shape),
    )


def solution(mesh):
    fine = jax.sharding.Mesh(mesh.devices.reshape(tuple(SIZES.values())), tuple(SIZES))
    slabs = P(GX, GY, None, None)
    in_specs = (slabs, slabs, P(GX, GY, None, None, None), P(), P(), P(), P())
    out_specs = (slabs, slabs, P(), P(), P(), P())
    return jax.shard_map(body, mesh=fine, in_specs=in_specs, out_specs=out_specs, check_vma=False)
```

```python
import functools
import math

import jax
import jax.numpy as jnp
from jax import lax
from jax.experimental import pallas as pl
from jax.experimental.pallas import tpu as pltpu
from jax.sharding import PartitionSpec as P

C = 96
LANES = 128
SIDE = 8
TAPS = 27
SPAN = TAPS * LANES
OWN = 512
RIM = 800
HALF = 2048
F32 = jnp.float32
BF16 = jnp.bfloat16

VMEM_SPEC = pl.BlockSpec(memory_space=pltpu.VMEM)
SMEM_SPEC = pl.BlockSpec(memory_space=pltpu.SMEM)
HBM_SPEC = pl.BlockSpec(memory_space=pltpu.HBM)


def call(kernel, out_shape, specs, scratch=(), flops=0, moved=0, name=None, room=8):
    return pl.pallas_call(
        kernel,
        out_shape=out_shape,
        in_specs=specs,
        out_specs=jax.tree.map(lambda _: VMEM_SPEC, out_shape),
        scratch_shapes=list(scratch),
        cost_estimate=pl.CostEstimate(flops=flops, bytes_accessed=moved, transcendentals=0),
        name=name,
        compiler_params=pltpu.CompilerParams(vmem_limit_bytes=room << 20),
    )


def sublane_low(shape):
    return lax.broadcasted_iota(jnp.int32, shape, len(shape) - 2) < 4


def rotated(value, shift):
    flat = value.reshape((-1,) + value.shape[-2:])
    return pltpu.roll(flat, shift, 1).reshape(value.shape)


def far(*arrays):
    return [pltpu.with_memory_space_constraint(array, pltpu.HBM) for array in arrays]


def started(pairs, sems):
    copies = [pltpu.make_async_copy(*pair, sems.at[n]) for n, pair in enumerate(pairs)]
    for copy in copies:
        copy.start()
    return copies


def grid_kernel(
    slots_far, features_far, cotangent_far, grid, low, high,
    lines, slots, features, cotangent, sems,
):
    copies = started(
        ((features_far, features), (cotangent_far, cotangent), (slots_far, slots)), sems
    )
    copies[2].wait()
    lane = lax.broadcasted_iota(jnp.int32, (16, 4, LANES), 2)
    spot = lax.broadcasted_iota(jnp.int32, (16, SIDE, LANES), 1)
    for field, source in enumerate((features, cotangent)):
        copies[field].wait()
        whole = source[0, 0].astype(F32)

        def tiles(part):
            starts = [(3 * line + part) * LANES for line in range(16)]
            return jnp.stack([whole[:, at : at + LANES] for at in starts], axis=0)

        first, middle, last = tiles(0), tiles(1), tiles(2)
        voxels = (
            first,
            jnp.where(lane < 32, moved_lanes(first, 32), moved_lanes(middle, 32)),
            jnp.where(lane < 64, moved_lanes(middle, 64), moved_lanes(last, 64)),
            moved_lanes(last, 96),
        )
        for w in range(4):
            lines[w] = jnp.zeros((16, SIDE, LANES), F32)
            lines[w, :, 0:4] = jnp.where(lane < C, voxels[w], 1.0 - field)
        for i in range(2):
            for j in range(2):
                tile = None
                for z in range(SIDE):
                    row = lines[z % 4, :, pl.ds(slots[0, 0, i, j, z // 4], 1)]
                    row = jnp.broadcast_to(row, (16, SIDE, LANES))
                    tile = row if tile is None else jnp.where(spot == z, row, tile)
                grid[field, 4 * i : 4 * i + 4, 4 * j : 4 * j + 4] = tile.reshape(4, 4, SIDE, LANES)
    for field in range(2):
        rows = slice(field * 128, field * 128 + 128)
        low[rows] = grid[field, 0:2].reshape(128, LANES).astype(BF16)
        high[rows] = grid[field, 6:8].reshape(128, LANES).astype(BF16)


def moved_lanes(value, shift):
    return pltpu.roll(value.reshape(64, LANES), shift, 1).reshape(16, 4, LANES)


def opened(message, lead):
    return message.astype(F32).reshape(lead + (SIDE, LANES))


def rim_kernel(grid, below, above, low, high):
    lower = opened(below[...], (2, 2, SIDE))
    upper = opened(above[...], (2, 2, SIDE))
    for message, at in ((low, 0), (high, SIDE - 2)):
        for field in range(2):
            base = field * 192
            message[base : base + 32] = (
                lower[field, :, at : at + 2].reshape(32, LANES).astype(BF16)
            )
            message[base + 32 : base + 160] = (
                grid[field, :, at : at + 2].reshape(128, LANES).astype(BF16)
            )
            message[base + 160 : base + 192] = (
                upper[field, :, at : at + 2].reshape(32, LANES).astype(BF16)
            )


def with_neighbours(value):
    spot = lax.broadcasted_iota(jnp.int32, value.shape, value.ndim - 2)
    before = jnp.where(spot == 0, 0.0, rotated(value, 1))
    after = jnp.where(spot == SIDE - 1, 0.0, rotated(value, SIDE - 1))
    return jnp.concatenate([before, value, after], axis=value.ndim - 1)


def fill_windows(windows, stacked, start, extent):
    rows = extent * extent * SIDE
    for wx in range(3):
        for wy in range(3):
            at = (wx * 3 + wy) * 3 * LANES
            piece = stacked[
                start + wx : start + wx + extent, start + wy : start + wy + extent
            ]
            windows[0:rows, at : at + 3 * LANES] = piece.reshape(rows, 3 * LANES).astype(BF16)


def spread(kernel, rows_ref):
    rows_ref[...] = jnp.zeros_like(rows_ref)
    for tap in range(TAPS):
        rows_ref[tap * LANES : tap * LANES + C, 0:C] = kernel[tap]


def spread_flipped(kernel, columns_ref):
    columns_ref[...] = jnp.zeros_like(columns_ref)
    for tap in range(TAPS):
        columns_ref[0:C, tap * LANES : tap * LANES + C] = kernel[TAPS - 1 - tap]


def plain_dot(left, right):
    return jnp.dot(left, right, preferred_element_type=F32)


def turned_dot(left, right):
    return lax.dot_general(left, right, (((1,), (1,)), ((), ())), preferred_element_type=F32)


def rounded(value):
    return value.astype(BF16).astype(F32)


def gradient_kernel(
    side, grid, below, above, left, right, one_far, two_far, gain_far, bias_far,
    keep, send, inner,
    field_ref, stack_ref, windows, terms_one, terms_two, packed_all,
    rows_ref, columns_ref, weight_one, weight_two, gain_ref, bias_ref, sems,
):
    copies = started(
        ((one_far, weight_one), (two_far, weight_two), (gain_far, gain_ref), (bias_far, bias_ref)), sems
    )
    lower = opened(below[...], (2, 2, SIDE))
    upper = opened(above[...], (2, 2, SIDE))
    to_left = opened(left[...], (2, SIDE + 4, 2))
    to_right = opened(right[...], (2, SIDE + 4, 2))

    def load_field(field):
        field_ref[2 : SIDE + 2, 2 : SIDE + 2] = grid[field]
        field_ref[0:2, 2 : SIDE + 2] = lower[field]
        field_ref[SIDE + 2 : SIDE + 4, 2 : SIDE + 2] = upper[field]
        field_ref[:, 0:2] = to_left[field]
        field_ref[:, SIDE + 2 : SIDE + 4] = to_right[field]

    load_field(0)
    mark = field_ref[1 : SIDE + 3, 1 : SIDE + 3].reshape(RIM, LANES)[:, C : C + 1]
    stack_ref[...] = with_neighbours(field_ref[...])
    fill_windows(windows, stack_ref, 0, SIDE + 2)
    for copy in copies:
        copy.wait()
    spread(weight_one, rows_ref)
    spread_flipped(weight_two, columns_ref)
    blank = jnp.zeros((1, LANES - C), F32)
    gain = jnp.concatenate([gain_ref[...], blank], axis=1)
    bias = jnp.concatenate([bias_ref[...], blank], axis=1)
    first_conv = plain_dot(windows[...], rows_ref[...]) * mark
    pre = first_conv * gain + bias
    gate = 1.0 / (1.0 + jnp.exp(-pre))
    hidden = rounded(pre * gate * mark)
    slope = gate * (1.0 + pre * (1.0 - gate)) * mark
    inner[0:RIM] = hidden.astype(BF16)

    load_field(1)
    stack_ref[...] = with_neighbours(field_ref[...])
    fill_windows(windows, stack_ref, 0, SIDE + 2)
    back_hidden = turned_dot(windows[...], columns_ref[...])
    back_pre = back_hidden * slope
    back_conv = rounded(back_pre * gain)
    inner[RIM : 2 * RIM] = back_conv.astype(BF16)

    def own(value):
        lead = value.reshape(SIDE + 2, SIDE + 2, SIDE, LANES)
        return lead[1 : SIDE + 1, 1 : SIDE + 1].reshape(OWN, LANES)

    own_pre = own(back_pre)
    gain_term = jnp.sum(own_pre * own(first_conv), axis=0, keepdims=True)
    bias_term = jnp.sum(own_pre, axis=0, keepdims=True)

    fill_windows(windows, stack_ref, 1, SIDE)
    hidden_turned = own(hidden).T.astype(BF16)
    terms_two[...] = plain_dot(hidden_turned, windows[0:OWN])

    lead = back_conv.reshape(SIDE + 2, SIDE + 2, SIDE, LANES)
    stack_ref[0 : SIDE + 2, 0 : SIDE + 2] = with_neighbours(lead)
    fill_windows(windows, stack_ref, 0, SIDE)
    features_turned = grid[0].reshape(OWN, LANES).T.astype(BF16)
    terms_one[...] = plain_dot(features_turned, windows[0:OWN])

    lane = lax.broadcasted_iota(jnp.int32, (C, LANES), 1)
    for terms, packed in ((terms_one, packed_all.at[0]), (terms_two, packed_all.at[1])):

        def term(tap):
            at = (TAPS - 1 - tap) * LANES
            return terms[0:C, at : at + LANES]

        for group in range(6):
            split = term(4 * group + 3)
            for part in range(3):
                row = (3 * group + part) * C
                moved = pltpu.roll(split, C - 32 * part, 1)
                joined = jnp.where(lane < C, term(4 * group + part), moved)
                packed[row : row + C] = joined
        for tap in range(24, TAPS):
            packed[(tap - 6) * C : (tap - 5) * C] = term(tap)
    blank = jnp.zeros((HALF - 21 * C - 2, LANES), F32)
    packed_all[0, 21 * C : HALF] = jnp.zeros((HALF - 21 * C, LANES), F32)
    packed_all[1, 21 * C : HALF] = jnp.concatenate([gain_term, bias_term, blank], axis=0)
    keep[...] = packed_all[side[0]]
    send[...] = packed_all[1 - side[0]]


def output_kernel(
    slots, grid, inner, one_far, two_far, out, grad,
    stack_ref, windows, rows_ref, columns_ref, weight_one, weight_two, sems,
):
    copies = started(((one_far, weight_one), (two_far, weight_two)), sems)
    for copy in copies:
        copy.wait()
    spread(weight_two, rows_ref)
    spread_flipped(weight_one, columns_ref)
    count = out.shape[0]
    out[...] = jnp.zeros_like(out)
    grad[...] = jnp.zeros_like(grad)
    for field, target in enumerate((out, grad)):
        lead = inner[field * RIM : field * RIM + RIM].astype(F32)
        stack_ref[...] = with_neighbours(lead.reshape(SIDE + 2, SIDE + 2, SIDE, LANES))
        fill_windows(windows, stack_ref, 0, SIDE)
        if field == 0:
            total = plain_dot(windows[...], rows_ref[...])
        else:
            total = turned_dot(windows[...], columns_ref[...])
        dense = total.reshape(SIDE, SIDE, SIDE, LANES) + grid[field]
        for i in range(2):
            for j in range(2):
                column = dense[4 * i : 4 * i + 4, 4 * j : 4 * j + 4].reshape(4, 2, 2, 8, LANES)
                even = column[:, :, 0].reshape(8, 8, LANES)
                odd = column[:, :, 1].reshape(8, 8, LANES)
                is_low = sublane_low(even.shape)
                tiles = (
                    jnp.where(is_low, even, rotated(odd, 4)),
                    jnp.where(is_low, rotated(even, 4), odd),
                )
                for k in range(2):
                    slot = slots[0, 0, i, j, k]
                    brick = tiles[k].reshape(64, LANES)[:, 0:C].astype(BF16)

                    @pl.when(slot < count)
                    def _():
                        target[slot] = brick


def unpack(scale, parts, grad):
    lane = lax.broadcasted_iota(jnp.int32, (C, LANES), 1)
    for group in range(6):
        held = [
            parts[(3 * group + part) * C : (3 * group + part + 1) * C].astype(F32) * scale
            for part in range(3)
        ]
        for part in range(3):
            grad[4 * group + part] = held[part][:, 0:C]
        moved = [pltpu.roll(held[part], 32 * part + 32, 1) for part in range(3)]
        last = jnp.where(lane < 32, moved[0], jnp.where(lane < 64, moved[1], moved[2]))
        grad[4 * group + 3] = last[:, 0:C]
    for tap in range(24, TAPS):
        grad[tap] = parts[(tap - 6) * C : (tap - 5) * C].astype(F32)[:, 0:C] * scale


def finish_kernel(scale, side, mine, other, grad_one, grad_two, grad_gain, grad_bias, parts):
    parts[side[0]] = mine[...]
    parts[1 - side[0]] = other[...]
    unpack(scale, parts.at[0], grad_one)
    unpack(scale, parts.at[1], grad_two)
    rest = parts[1, 21 * C : HALF].astype(F32) * scale
    grad_gain[...] = rest[0:1, 0:C]
    grad_bias[...] = rest[1:2, 0:C]


def shape(dims, dtype):
    return jax.ShapeDtypeStruct(dims, dtype)


def dense_parts(features, cotangent, slots):
    return call(
        grid_kernel,
        (shape((2, SIDE, SIDE, SIDE, LANES), F32), shape((256, LANES), BF16), shape((256, LANES), BF16)),
        [HBM_SPEC] * 3,
        scratch=[
            pltpu.VMEM((4, 16, SIDE, LANES), F32),
            pltpu.SMEM(slots.shape, jnp.int32),
            pltpu.VMEM(features.shape, BF16),
            pltpu.VMEM(features.shape, BF16),
            pltpu.SemaphoreType.DMA((3,)),
        ],
        moved=2_000_000,
        name="dense_grid",
    )(*far(slots, features, cotangent))


def rims(grid, below, above):
    return call(
        rim_kernel,
        (shape((384, LANES), BF16), shape((384, LANES), BF16)),
        [VMEM_SPEC] * 3,
        moved=1_500_000,
        name="rims",
    )(grid, below, above)


def weight_scratch():
    return [
        pltpu.VMEM((SPAN, LANES), BF16),
        pltpu.VMEM((LANES, SPAN), BF16),
        pltpu.VMEM((TAPS, C, C), BF16),
        pltpu.VMEM((TAPS, C, C), BF16),
    ]


def gradients(side, grid, halos, weight_one, weight_two, gain, bias):
    return call(
        gradient_kernel,
        (shape((HALF, LANES), F32), shape((HALF, LANES), F32), shape((2 * RIM, LANES), BF16)),
        [SMEM_SPEC] + [VMEM_SPEC] * 5 + [HBM_SPEC] * 4,
        scratch=[
            pltpu.VMEM((SIDE + 4, SIDE + 4, SIDE, LANES), F32),
            pltpu.VMEM((SIDE + 4, SIDE + 4, SIDE, 3 * LANES), F32),
            pltpu.VMEM((RIM, SPAN), BF16),
            pltpu.VMEM((LANES, SPAN), F32),
            pltpu.VMEM((LANES, SPAN), F32),
            pltpu.VMEM((2, HALF, LANES), F32),
            *weight_scratch(),
            pltpu.VMEM((1, C), F32),
            pltpu.VMEM((1, C), F32),
            pltpu.SemaphoreType.DMA((4,)),
        ],
        flops=2_400_000_000,
        moved=8_000_000,
        name="gradients",
        room=28,
    )(side, grid, *halos, *far(weight_one, weight_two, gain.reshape(1, C), bias.reshape(1, C)))


def outputs(slots, grid, inner, weight_one, weight_two):
    result = shape((4, 64, C), BF16)
    return call(
        output_kernel,
        (result, result),
        [SMEM_SPEC] + [VMEM_SPEC] * 2 + [HBM_SPEC] * 2,
        scratch=[
            pltpu.VMEM((SIDE + 2, SIDE + 2, SIDE, 3 * LANES), F32),
            pltpu.VMEM((OWN, SPAN), BF16),
            *weight_scratch(),
            pltpu.SemaphoreType.DMA((2,)),
        ],
        flops=900_000_000,
        moved=4_000_000,
        name="outputs",
        room=18,
    )(slots, grid, inner, *far(weight_one, weight_two))


def finish(side, mine, other, scale):
    grads, line = shape((TAPS, C, C), F32), shape((1, C), F32)
    return call(
        functools.partial(finish_kernel, scale),
        (grads, grads, line, line),
        [SMEM_SPEC, VMEM_SPEC, VMEM_SPEC],
        scratch=[pltpu.VMEM((2, HALF, LANES), BF16)],
        moved=4_000_000,
        name="finish",
    )(side, mine, other)


SIZES = dict(y=4, zh=4, core=2, zl=2, zp=2, x=4)
PLANE = ("y", "x", "zp")
LINE = ("zh", "zl")


def spread_out(block, axes):
    copies = jnp.broadcast_to(block, (lax.axis_size(axes),) + block.shape)
    return lax.all_to_all(copies, axes, 0, 0)


def other_core(block):
    return lax.ppermute(block, "core", [(0, 1), (1, 0)])


def reduce_all(keep, send):
    pair = (keep + other_core(send)).astype(BF16)
    parts = lax.all_to_all(pair.reshape(lax.axis_size(PLANE), -1, LANES), PLANE, 0, 0)
    chunk = jnp.sum(parts.astype(F32), axis=0)
    chunk = jnp.sum(spread_out(chunk, LINE), axis=0)
    return spread_out(chunk.astype(BF16), PLANE).reshape(HALF, LANES)


GX = ("y", "zh", "core")
GY = ("zl", "zp", "x")


def passed_along(block, axis, distance):
    devices = range(lax.axis_size(axis))
    route = [(i - distance, i) for i in devices if i - distance in devices]
    return lax.ppermute(block, axis, route)


def body(features, cotangent, brick_slot, weight_one, weight_two, gain, bias):
    side = lax.axis_index("core").reshape(1)
    grid, low, high = dense_parts(features, cotangent, brick_slot)
    below = passed_along(high, GX, 1)
    above = passed_along(low, GX, -1)
    low, high = rims(grid, below, above)
    left = passed_along(high, GY, 1)
    right = passed_along(low, GY, -1)
    keep, send, inner = gradients(side, grid, (below, above, left, right), weight_one, weight_two, gain, bias)
    out, grad = outputs(brick_slot, grid, inner, weight_one, weight_two)
    out, grad = out.reshape(features.shape), grad.reshape(features.shape)
    mine, out, grad = lax.optimization_barrier((reduce_all(keep, send), out, grad))
    other = other_core(mine)
    scale = 1.0 / math.sqrt(lax.axis_size(GX) * lax.axis_size(GY) * 256)
    grad_one, grad_two, grad_gain, grad_bias = finish(side, mine, other, scale)
    return (
        out,
        grad,
        grad_one,
        grad_two,
        grad_gain.reshape(gain.shape),
        grad_bias.reshape(bias.shape),
    )


def solution(mesh):
    fine = jax.sharding.Mesh(mesh.devices.reshape(tuple(SIZES.values())), tuple(SIZES))
    slabs = P(GX, GY, None, None)
    in_specs = (slabs, slabs, P(GX, GY, None, None, None), P(), P(), P(), P())
    out_specs = (slabs, slabs, P(), P(), P(), P())
    return jax.shard_map(body, mesh=fine, in_specs=in_specs, out_specs=out_specs, check_vma=False)
```

```python
import functools
import math

import jax
import jax.numpy as jnp
from jax import lax
from jax.experimental import pallas as pl
from jax.experimental.pallas import tpu as pltpu
from jax.sharding import PartitionSpec as P

C = 96
LANES = 128
SIDE = 8
TAPS = 27
SPAN = TAPS * LANES
OWN = 512
RIM = 800
HALF = 2048
F32 = jnp.float32
BF16 = jnp.bfloat16

VMEM_SPEC = pl.BlockSpec(memory_space=pltpu.VMEM)
SMEM_SPEC = pl.BlockSpec(memory_space=pltpu.SMEM)
HBM_SPEC = pl.BlockSpec(memory_space=pltpu.HBM)


def call(kernel, out_shape, specs, scratch=(), flops=0, moved=0, name=None, room=8):
    return pl.pallas_call(
        kernel,
        out_shape=out_shape,
        in_specs=specs,
        out_specs=jax.tree.map(lambda _: VMEM_SPEC, out_shape),
        scratch_shapes=list(scratch),
        cost_estimate=pl.CostEstimate(flops=flops, bytes_accessed=moved, transcendentals=0),
        name=name,
        compiler_params=pltpu.CompilerParams(vmem_limit_bytes=room << 20),
    )


def sublane_low(shape):
    return lax.broadcasted_iota(jnp.int32, shape, len(shape) - 2) < 4


def rotated(value, shift):
    flat = value.reshape((-1,) + value.shape[-2:])
    return pltpu.roll(flat, shift, 1).reshape(value.shape)


def kept_far(*arrays):
    return [pltpu.with_memory_space_constraint(array, pltpu.HBM) for array in arrays]


def started(pairs, sems):
    copies = [pltpu.make_async_copy(*pair, sems.at[n]) for n, pair in enumerate(pairs)]
    for copy in copies:
        copy.start()
    return copies


def grid_kernel(
    sides, slots_far, features_far, cotangent_far, grid, far, near,
    lines, slots, features, cotangent, sems,
):
    copies = started(
        ((features_far, features), (cotangent_far, cotangent), (slots_far, slots)), sems
    )
    copies[2].wait()
    lane = lax.broadcasted_iota(jnp.int32, (16, 4, LANES), 2)
    spot = lax.broadcasted_iota(jnp.int32, (16, SIDE, LANES), 1)
    for field, source in enumerate((features, cotangent)):
        copies[field].wait()
        whole = source[0, 0].astype(F32)

        def tiles(part):
            starts = [(3 * line + part) * LANES for line in range(16)]
            return jnp.stack([whole[:, at : at + LANES] for at in starts], axis=0)

        first, middle, last = tiles(0), tiles(1), tiles(2)
        voxels = (
            first,
            jnp.where(lane < 32, moved_lanes(first, 32), moved_lanes(middle, 32)),
            jnp.where(lane < 64, moved_lanes(middle, 64), moved_lanes(last, 64)),
            moved_lanes(last, 96),
        )
        for w in range(4):
            lines[w] = jnp.zeros((16, SIDE, LANES), F32)
            lines[w, :, 0:4] = jnp.where(lane < C, voxels[w], 1.0 - field)
        for i in range(2):
            for j in range(2):
                tile = None
                for z in range(SIDE):
                    row = lines[z % 4, :, pl.ds(slots[0, 0, i, j, z // 4], 1)]
                    row = jnp.broadcast_to(row, (16, SIDE, LANES))
                    tile = row if tile is None else jnp.where(spot == z, row, tile)
                grid[field, 4 * i : 4 * i + 4, 4 * j : 4 * j + 4] = tile.reshape(4, 4, SIDE, LANES)
    for field in range(2):
        rows = slice(field * 128, field * 128 + 128)
        for message, at in ((near, 6 - 6 * sides[0]), (far, 6 * sides[0])):
            message[rows] = grid[field, pl.ds(at, 2)].reshape(128, LANES).astype(BF16)


def moved_lanes(value, shift):
    return pltpu.roll(value.reshape(64, LANES), shift, 1).reshape(16, 4, LANES)


def opened(message, lead):
    return message.astype(F32).reshape(lead + (SIDE, LANES))


def lower_upper(side, near, far, lead):
    near, far = opened(near[...], lead), opened(far[...], lead)
    even = side == 0
    return jnp.where(even, far, near), jnp.where(even, near, far)


def rim_kernel(sides, grid, far_x, near_x, far, near):
    lower, upper = lower_upper(sides[0], near_x, far_x, (2, 2, SIDE))
    even = sides[1] == 0

    def picked(block, message):
        first, last = block[:, 0:2], block[:, SIDE - 2 : SIDE]
        chosen = jnp.where(even, last, first) if message is near else jnp.where(even, first, last)
        return chosen.reshape(32, LANES).astype(BF16)

    for message, at in ((near, 6 - 6 * sides[1]), (far, 6 * sides[1])):
        for field in range(2):
            base = field * 192
            message[base : base + 32] = picked(lower[field], message)
            own = grid[field, :, pl.ds(at, 2)].reshape(128, LANES)
            message[base + 32 : base + 160] = own.astype(BF16)
            message[base + 160 : base + 192] = picked(upper[field], message)


def with_neighbours(value):
    spot = lax.broadcasted_iota(jnp.int32, value.shape, value.ndim - 2)
    before = jnp.where(spot == 0, 0.0, rotated(value, 1))
    after = jnp.where(spot == SIDE - 1, 0.0, rotated(value, SIDE - 1))
    return jnp.concatenate([before, value, after], axis=value.ndim - 1)


def fill_windows(windows, stacked, start, extent):
    rows = extent * extent * SIDE
    for wx in range(3):
        for wy in range(3):
            at = (wx * 3 + wy) * 3 * LANES
            piece = stacked[
                start + wx : start + wx + extent, start + wy : start + wy + extent
            ]
            windows[0:rows, at : at + 3 * LANES] = piece.reshape(rows, 3 * LANES).astype(BF16)


def spread(kernel, rows_ref):
    rows_ref[...] = jnp.zeros_like(rows_ref)
    for tap in range(TAPS):
        rows_ref[tap * LANES : tap * LANES + C, 0:C] = kernel[tap]


def spread_flipped(kernel, columns_ref):
    columns_ref[...] = jnp.zeros_like(columns_ref)
    for tap in range(TAPS):
        columns_ref[0:C, tap * LANES : tap * LANES + C] = kernel[TAPS - 1 - tap]


def plain_dot(left, right):
    return jnp.dot(left, right, preferred_element_type=F32)


def turned_dot(left, right):
    return lax.dot_general(left, right, (((1,), (1,)), ((), ())), preferred_element_type=F32)


def rounded(value):
    return value.astype(BF16).astype(F32)


def gradient_kernel(
    sides, grid, far_x, near_x, far_y, near_y, one_far, two_far, gain_far, bias_far,
    keep, send, inner,
    field_ref, stack_ref, windows, terms_one, terms_two, packed_all,
    rows_ref, columns_ref, weight_one, weight_two, gain_ref, bias_ref, sems,
):
    copies = started(
        ((one_far, weight_one), (two_far, weight_two), (gain_far, gain_ref), (bias_far, bias_ref)), sems
    )
    lower, upper = lower_upper(sides[0], near_x, far_x, (2, 2, SIDE))
    to_left, to_right = lower_upper(sides[1], near_y, far_y, (2, SIDE + 4, 2))

    def load_field(field):
        field_ref[2 : SIDE + 2, 2 : SIDE + 2] = grid[field]
        field_ref[0:2, 2 : SIDE + 2] = lower[field]
        field_ref[SIDE + 2 : SIDE + 4, 2 : SIDE + 2] = upper[field]
        field_ref[:, 0:2] = to_left[field]
        field_ref[:, SIDE + 2 : SIDE + 4] = to_right[field]

    load_field(0)
    mark = field_ref[1 : SIDE + 3, 1 : SIDE + 3].reshape(RIM, LANES)[:, C : C + 1]
    stack_ref[...] = with_neighbours(field_ref[...])
    fill_windows(windows, stack_ref, 0, SIDE + 2)
    for copy in copies:
        copy.wait()
    spread(weight_one, rows_ref)
    spread_flipped(weight_two, columns_ref)
    blank = jnp.zeros((1, LANES - C), F32)
    gain = jnp.concatenate([gain_ref[...], blank], axis=1)
    bias = jnp.concatenate([bias_ref[...], blank], axis=1)
    first_conv = plain_dot(windows[...], rows_ref[...]) * mark
    pre = first_conv * gain + bias
    gate = 1.0 / (1.0 + jnp.exp(-pre))
    hidden = rounded(pre * gate * mark)
    slope = gate * (1.0 + pre * (1.0 - gate)) * mark
    inner[0:RIM] = hidden.astype(BF16)

    load_field(1)
    stack_ref[...] = with_neighbours(field_ref[...])
    fill_windows(windows, stack_ref, 0, SIDE + 2)
    back_hidden = turned_dot(windows[...], columns_ref[...])
    back_pre = back_hidden * slope
    back_conv = rounded(back_pre * gain)
    inner[RIM : 2 * RIM] = back_conv.astype(BF16)

    def own(value):
        lead = value.reshape(SIDE + 2, SIDE + 2, SIDE, LANES)
        return lead[1 : SIDE + 1, 1 : SIDE + 1].reshape(OWN, LANES)

    own_pre = own(back_pre)
    gain_term = jnp.sum(own_pre * own(first_conv), axis=0, keepdims=True)
    bias_term = jnp.sum(own_pre, axis=0, keepdims=True)

    fill_windows(windows, stack_ref, 1, SIDE)
    hidden_turned = own(hidden).T.astype(BF16)
    terms_two[...] = plain_dot(hidden_turned, windows[0:OWN])

    lead = back_conv.reshape(SIDE + 2, SIDE + 2, SIDE, LANES)
    stack_ref[0 : SIDE + 2, 0 : SIDE + 2] = with_neighbours(lead)
    fill_windows(windows, stack_ref, 0, SIDE)
    features_turned = grid[0].reshape(OWN, LANES).T.astype(BF16)
    terms_one[...] = plain_dot(features_turned, windows[0:OWN])

    lane = lax.broadcasted_iota(jnp.int32, (C, LANES), 1)
    for terms, packed in ((terms_one, packed_all.at[0]), (terms_two, packed_all.at[1])):

        def term(tap):
            at = (TAPS - 1 - tap) * LANES
            return terms[0:C, at : at + LANES]

        for group in range(6):
            split = term(4 * group + 3)
            for part in range(3):
                row = (3 * group + part) * C
                moved = pltpu.roll(split, C - 32 * part, 1)
                joined = jnp.where(lane < C, term(4 * group + part), moved)
                packed[row : row + C] = joined
        for tap in range(24, TAPS):
            packed[(tap - 6) * C : (tap - 5) * C] = term(tap)
    blank = jnp.zeros((HALF - 21 * C - 2, LANES), F32)
    packed_all[0, 21 * C : HALF] = jnp.zeros((HALF - 21 * C, LANES), F32)
    packed_all[1, 21 * C : HALF] = jnp.concatenate([gain_term, bias_term, blank], axis=0)
    keep[...] = packed_all[sides[0]]
    send[...] = packed_all[1 - sides[0]]


def output_kernel(
    slots, grid, inner, one_far, two_far, out, grad,
    stack_ref, windows, rows_ref, columns_ref, weight_one, weight_two, sems,
):
    copies = started(((one_far, weight_one), (two_far, weight_two)), sems)
    for copy in copies:
        copy.wait()
    spread(weight_two, rows_ref)
    spread_flipped(weight_one, columns_ref)
    count = out.shape[0]
    out[...] = jnp.zeros_like(out)
    grad[...] = jnp.zeros_like(grad)
    for field, target in enumerate((out, grad)):
        lead = inner[field * RIM : field * RIM + RIM].astype(F32)
        stack_ref[...] = with_neighbours(lead.reshape(SIDE + 2, SIDE + 2, SIDE, LANES))
        fill_windows(windows, stack_ref, 0, SIDE)
        if field == 0:
            total = plain_dot(windows[...], rows_ref[...])
        else:
            total = turned_dot(windows[...], columns_ref[...])
        dense = total.reshape(SIDE, SIDE, SIDE, LANES) + grid[field]
        for i in range(2):
            for j in range(2):
                column = dense[4 * i : 4 * i + 4, 4 * j : 4 * j + 4].reshape(4, 2, 2, 8, LANES)
                even = column[:, :, 0].reshape(8, 8, LANES)
                odd = column[:, :, 1].reshape(8, 8, LANES)
                is_low = sublane_low(even.shape)
                tiles = (
                    jnp.where(is_low, even, rotated(odd, 4)),
                    jnp.where(is_low, rotated(even, 4), odd),
                )
                for k in range(2):
                    slot = slots[0, 0, i, j, k]
                    brick = tiles[k].reshape(64, LANES)[:, 0:C].astype(BF16)

                    @pl.when(slot < count)
                    def _():
                        target[slot] = brick


def unpack(scale, parts, grad):
    lane = lax.broadcasted_iota(jnp.int32, (C, LANES), 1)
    for group in range(6):
        held = [
            parts[(3 * group + part) * C : (3 * group + part + 1) * C].astype(F32) * scale
            for part in range(3)
        ]
        for part in range(3):
            grad[4 * group + part] = held[part][:, 0:C]
        moved = [pltpu.roll(held[part], 32 * part + 32, 1) for part in range(3)]
        last = jnp.where(lane < 32, moved[0], jnp.where(lane < 64, moved[1], moved[2]))
        grad[4 * group + 3] = last[:, 0:C]
    for tap in range(24, TAPS):
        grad[tap] = parts[(tap - 6) * C : (tap - 5) * C].astype(F32)[:, 0:C] * scale


def finish_kernel(scale, sides, mine, other, grad_one, grad_two, grad_gain, grad_bias, parts):
    parts[sides[0]] = mine[...]
    parts[1 - sides[0]] = other[...]
    unpack(scale, parts.at[0], grad_one)
    unpack(scale, parts.at[1], grad_two)
    rest = parts[1, 21 * C : HALF].astype(F32) * scale
    grad_gain[...] = rest[0:1, 0:C]
    grad_bias[...] = rest[1:2, 0:C]


def shape(dims, dtype):
    return jax.ShapeDtypeStruct(dims, dtype)


def dense_parts(sides, features, cotangent, slots):
    return call(
        grid_kernel,
        (shape((2, SIDE, SIDE, SIDE, LANES), F32), shape((256, LANES), BF16), shape((256, LANES), BF16)),
        [SMEM_SPEC] + [HBM_SPEC] * 3,
        scratch=[
            pltpu.VMEM((4, 16, SIDE, LANES), F32),
            pltpu.SMEM(slots.shape, jnp.int32),
            pltpu.VMEM(features.shape, BF16),
            pltpu.VMEM(features.shape, BF16),
            pltpu.SemaphoreType.DMA((3,)),
        ],
        moved=2_000_000,
        name="dense_grid",
    )(sides, *kept_far(slots, features, cotangent))


def rims(sides, grid, far_x, near_x):
    return call(
        rim_kernel,
        (shape((384, LANES), BF16), shape((384, LANES), BF16)),
        [SMEM_SPEC] + [VMEM_SPEC] * 3,
        moved=1_500_000,
        name="rims",
    )(sides, grid, far_x, near_x)


def weight_scratch():
    return [
        pltpu.VMEM((SPAN, LANES), BF16),
        pltpu.VMEM((LANES, SPAN), BF16),
        pltpu.VMEM((TAPS, C, C), BF16),
        pltpu.VMEM((TAPS, C, C), BF16),
    ]


def gradients(side, grid, halos, weight_one, weight_two, gain, bias):
    return call(
        gradient_kernel,
        (shape((HALF, LANES), F32), shape((HALF, LANES), F32), shape((2 * RIM, LANES), BF16)),
        [SMEM_SPEC] + [VMEM_SPEC] * 5 + [HBM_SPEC] * 4,
        scratch=[
            pltpu.VMEM((SIDE + 4, SIDE + 4, SIDE, LANES), F32),
            pltpu.VMEM((SIDE + 4, SIDE + 4, SIDE, 3 * LANES), F32),
            pltpu.VMEM((RIM, SPAN), BF16),
            pltpu.VMEM((LANES, SPAN), F32),
            pltpu.VMEM((LANES, SPAN), F32),
            pltpu.VMEM((2, HALF, LANES), F32),
            *weight_scratch(),
            pltpu.VMEM((1, C), F32),
            pltpu.VMEM((1, C), F32),
            pltpu.SemaphoreType.DMA((4,)),
        ],
        flops=2_400_000_000,
        moved=8_000_000,
        name="gradients",
        room=28,
    )(side, grid, *halos, *kept_far(weight_one, weight_two, gain.reshape(1, C), bias.reshape(1, C)))


def outputs(slots, grid, inner, weight_one, weight_two):
    result = shape((4, 64, C), BF16)
    return call(
        output_kernel,
        (result, result),
        [SMEM_SPEC] + [VMEM_SPEC] * 2 + [HBM_SPEC] * 2,
        scratch=[
            pltpu.VMEM((SIDE + 2, SIDE + 2, SIDE, 3 * LANES), F32),
            pltpu.VMEM((OWN, SPAN), BF16),
            *weight_scratch(),
            pltpu.SemaphoreType.DMA((2,)),
        ],
        flops=900_000_000,
        moved=4_000_000,
        name="outputs",
        room=18,
    )(slots, grid, inner, *kept_far(weight_one, weight_two))


def finish(side, mine, other, scale):
    grads, line = shape((TAPS, C, C), F32), shape((1, C), F32)
    return call(
        functools.partial(finish_kernel, scale),
        (grads, grads, line, line),
        [SMEM_SPEC, VMEM_SPEC, VMEM_SPEC],
        scratch=[pltpu.VMEM((2, HALF, LANES), BF16)],
        moved=4_000_000,
        name="finish",
    )(side, mine, other)


SIZES = dict(y=4, zh=4, core=2, zl=2, zp=2, x=4)
PLANE = ("y", "x", "zp")
LINE = ("zh", "zl")


def spread_out(block, axes):
    copies = jnp.broadcast_to(block, (lax.axis_size(axes),) + block.shape)
    return lax.all_to_all(copies, axes, 0, 0)


def other_core(block):
    return lax.ppermute(block, "core", [(0, 1), (1, 0)])


def reduce_all(keep, send, beside):
    pair = (keep + other_core(send)).astype(BF16)
    parts = lax.all_to_all(pair.reshape(lax.axis_size(PLANE), -1, LANES), PLANE, 0, 0)
    chunk = jnp.sum(parts.astype(F32), axis=0)
    chunks, beside = lax.optimization_barrier((spread_out(chunk, LINE), beside))
    chunk = jnp.sum(chunks, axis=0)
    return spread_out(chunk.astype(BF16), PLANE).reshape(HALF, LANES), beside


GX = ("y", "zh", "core")
GY = ("zl", "zp", "x")


def swapped(far, near, axis):
    count = lax.axis_size(axis)
    ends = {n: n + 1 for n in range(1, count - 1, 2)}
    route = [pair for low, high in ends.items() for pair in ((low, high), (high, low))]
    far = lax.ppermute(far, axis, route)
    near = lax.ppermute(near, axis, [(n, n ^ 1) for n in range(count)])
    return far, near


def body(features, cotangent, brick_slot, weight_one, weight_two, gain, bias):
    sides = jnp.stack([lax.axis_index("core"), lax.axis_index("x") & 1])
    grid, far, near = dense_parts(sides, features, cotangent, brick_slot)
    around_x = swapped(far, near, GX)
    far, near = rims(sides, grid, *around_x)
    halos = (*around_x, *swapped(far, near, GY))
    keep, send, inner = gradients(sides, grid, halos, weight_one, weight_two, gain, bias)
    out, grad = outputs(brick_slot, grid, inner, weight_one, weight_two)
    out, grad = out.reshape(features.shape), grad.reshape(features.shape)
    mine, (out, grad) = reduce_all(keep, send, (out, grad))
    other = other_core(mine)
    scale = 1.0 / math.sqrt(lax.axis_size(GX) * lax.axis_size(GY) * 256)
    grad_one, grad_two, grad_gain, grad_bias = finish(sides, mine, other, scale)
    return (
        out,
        grad,
        grad_one,
        grad_two,
        grad_gain.reshape(gain.shape),
        grad_bias.reshape(bias.shape),
    )


def solution(mesh):
    fine = jax.sharding.Mesh(mesh.devices.reshape(tuple(SIZES.values())), tuple(SIZES))
    slabs = P(GX, GY, None, None)
    in_specs = (slabs, slabs, P(GX, GY, None, None, None), P(), P(), P(), P())
    out_specs = (slabs, slabs, P(), P(), P(), P())
    return jax.shard_map(body, mesh=fine, in_specs=in_specs, out_specs=out_specs, check_vma=False)
```

```python
import functools
import math

import jax
import jax.numpy as jnp
from jax import lax
from jax.experimental import pallas as pl
from jax.experimental.pallas import tpu as pltpu
from jax.sharding import PartitionSpec as P

C = 96
LANES = 128
SIDE = 8
TAPS = 27
SPAN = TAPS * LANES
OWN = 512
RIM = 800
HALF = 2048
F32 = jnp.float32
BF16 = jnp.bfloat16

VMEM_SPEC = pl.BlockSpec(memory_space=pltpu.VMEM)
SMEM_SPEC = pl.BlockSpec(memory_space=pltpu.SMEM)
HBM_SPEC = pl.BlockSpec(memory_space=pltpu.HBM)


def call(kernel, out_shape, specs, scratch=(), flops=0, moved=0, name=None, room=8):
    return pl.pallas_call(
        kernel,
        out_shape=out_shape,
        in_specs=specs,
        out_specs=jax.tree.map(lambda _: VMEM_SPEC, out_shape),
        scratch_shapes=list(scratch),
        cost_estimate=pl.CostEstimate(flops=flops, bytes_accessed=moved, transcendentals=0),
        name=name,
        compiler_params=pltpu.CompilerParams(vmem_limit_bytes=room << 20),
    )


def sublane_low(shape):
    return lax.broadcasted_iota(jnp.int32, shape, len(shape) - 2) < 4


def rotated(value, shift):
    flat = value.reshape((-1,) + value.shape[-2:])
    return pltpu.roll(flat, shift, 1).reshape(value.shape)


def kept_far(*arrays):
    return [pltpu.with_memory_space_constraint(array, pltpu.HBM) for array in arrays]


def started(pairs, sems):
    copies = [pltpu.make_async_copy(*pair, sems.at[n]) for n, pair in enumerate(pairs)]
    for copy in copies:
        copy.start()
    return copies


def grid_kernel(
    slots_far, features_far, cotangent_far, grid, far, near,
    lines, slots, features, cotangent, sems,
):
    copies = started(
        ((features_far, features), (cotangent_far, cotangent), (slots_far, slots)), sems
    )
    copies[2].wait()
    sides = parities()
    lane = lax.broadcasted_iota(jnp.int32, (16, 4, LANES), 2)
    spot = lax.broadcasted_iota(jnp.int32, (16, SIDE, LANES), 1)
    for field, source in enumerate((features, cotangent)):
        copies[field].wait()
        whole = source[0, 0].astype(F32)

        def tiles(part):
            starts = [(3 * line + part) * LANES for line in range(16)]
            return jnp.stack([whole[:, at : at + LANES] for at in starts], axis=0)

        first, middle, last = tiles(0), tiles(1), tiles(2)
        voxels = (
            first,
            jnp.where(lane < 32, moved_lanes(first, 32), moved_lanes(middle, 32)),
            jnp.where(lane < 64, moved_lanes(middle, 64), moved_lanes(last, 64)),
            moved_lanes(last, 96),
        )
        for w in range(4):
            lines[w] = jnp.zeros((16, SIDE, LANES), F32)
            lines[w, :, 0:4] = jnp.where(lane < C, voxels[w], 1.0 - field)
        for i in range(2):
            for j in range(2):
                tile = None
                for z in range(SIDE):
                    row = lines[z % 4, :, pl.ds(slots[0, 0, i, j, z // 4], 1)]
                    row = jnp.broadcast_to(row, (16, SIDE, LANES))
                    tile = row if tile is None else jnp.where(spot == z, row, tile)
                grid[field, 4 * i : 4 * i + 4, 4 * j : 4 * j + 4] = tile.reshape(4, 4, SIDE, LANES)
    for field in range(2):
        rows = slice(field * 128, field * 128 + 128)
        for message, at in ((near, 6 - 6 * sides[0]), (far, 6 * sides[0])):
            message[rows] = grid[field, pl.ds(at, 2)].reshape(128, LANES).astype(BF16)


def moved_lanes(value, shift):
    return pltpu.roll(value.reshape(64, LANES), shift, 1).reshape(16, 4, LANES)


def parities():
    return lax.axis_index("core"), lax.axis_index("x") & 1


def opened(message, lead):
    return message.astype(F32).reshape(lead + (SIDE, LANES))


def lower_upper(side, near, far, lead):
    near, far = opened(near[...], lead), opened(far[...], lead)
    even = side == 0
    return jnp.where(even, far, near), jnp.where(even, near, far)


def rim_kernel(grid, far_x, near_x, far, near):
    sides = parities()
    lower, upper = lower_upper(sides[0], near_x, far_x, (2, 2, SIDE))
    even = sides[1] == 0

    def picked(block, message):
        first, last = block[:, 0:2], block[:, SIDE - 2 : SIDE]
        chosen = jnp.where(even, last, first) if message is near else jnp.where(even, first, last)
        return chosen.reshape(32, LANES).astype(BF16)

    for message, at in ((near, 6 - 6 * sides[1]), (far, 6 * sides[1])):
        for field in range(2):
            base = field * 192
            message[base : base + 32] = picked(lower[field], message)
            own = grid[field, :, pl.ds(at, 2)].reshape(128, LANES)
            message[base + 32 : base + 160] = own.astype(BF16)
            message[base + 160 : base + 192] = picked(upper[field], message)


def with_neighbours(value):
    spot = lax.broadcasted_iota(jnp.int32, value.shape, value.ndim - 2)
    before = jnp.where(spot == 0, 0.0, rotated(value, 1))
    after = jnp.where(spot == SIDE - 1, 0.0, rotated(value, SIDE - 1))
    return jnp.concatenate([before, value, after], axis=value.ndim - 1)


def fill_windows(windows, stacked, start, extent):
    rows = extent * extent * SIDE
    for wx in range(3):
        for wy in range(3):
            at = (wx * 3 + wy) * 3 * LANES
            piece = stacked[
                start + wx : start + wx + extent, start + wy : start + wy + extent
            ]
            windows[0:rows, at : at + 3 * LANES] = piece.reshape(rows, 3 * LANES).astype(BF16)


def spread(kernel, rows_ref):
    rows_ref[...] = jnp.zeros_like(rows_ref)
    for tap in range(TAPS):
        rows_ref[tap * LANES : tap * LANES + C, 0:C] = kernel[tap]


def spread_flipped(kernel, columns_ref):
    columns_ref[...] = jnp.zeros_like(columns_ref)
    for tap in range(TAPS):
        columns_ref[0:C, tap * LANES : tap * LANES + C] = kernel[TAPS - 1 - tap]


def prepare_kernel(
    one_far, two_far, gain_far, bias_far, rows_ref, columns_ref, gain_bias,
    weight_one, weight_two, gain_ref, bias_ref, sems,
):
    copies = started(
        ((one_far, weight_one), (two_far, weight_two), (gain_far, gain_ref), (bias_far, bias_ref)), sems
    )
    for copy in copies:
        copy.wait()
    spread(weight_one, rows_ref)
    spread_flipped(weight_two, columns_ref)
    gain_bias[...] = jnp.zeros_like(gain_bias)
    gain_bias[0:1, 0:C] = gain_ref[...]
    gain_bias[1:2, 0:C] = bias_ref[...]


def plain_dot(left, right):
    return jnp.dot(left, right, preferred_element_type=F32)


def turned_dot(left, right):
    return lax.dot_general(left, right, (((1,), (1,)), ((), ())), preferred_element_type=F32)


def rounded(value):
    return value.astype(BF16).astype(F32)


def gradient_kernel(
    grid, far_x, near_x, far_y, near_y, rows_ref, columns_ref, gain_bias,
    keep, send, inner,
    field_ref, stack_ref, windows, terms_one, terms_two, packed_all,
):
    sides = parities()
    gain, bias = gain_bias[0:1], gain_bias[1:2]
    lower, upper = lower_upper(sides[0], near_x, far_x, (2, 2, SIDE))
    to_left, to_right = lower_upper(sides[1], near_y, far_y, (2, SIDE + 4, 2))

    def load_field(field):
        field_ref[2 : SIDE + 2, 2 : SIDE + 2] = grid[field]
        field_ref[0:2, 2 : SIDE + 2] = lower[field]
        field_ref[SIDE + 2 : SIDE + 4, 2 : SIDE + 2] = upper[field]
        field_ref[:, 0:2] = to_left[field]
        field_ref[:, SIDE + 2 : SIDE + 4] = to_right[field]

    load_field(0)
    mark = field_ref[1 : SIDE + 3, 1 : SIDE + 3].reshape(RIM, LANES)[:, C : C + 1]
    stack_ref[...] = with_neighbours(field_ref[...])
    fill_windows(windows, stack_ref, 0, SIDE + 2)
    first_conv = plain_dot(windows[...], rows_ref[...]) * mark
    pre = first_conv * gain + bias
    gate = 1.0 / (1.0 + jnp.exp(-pre))
    hidden = rounded(pre * gate * mark)
    slope = gate * (1.0 + pre * (1.0 - gate)) * mark
    inner[0:RIM] = hidden.astype(BF16)

    load_field(1)
    stack_ref[...] = with_neighbours(field_ref[...])
    fill_windows(windows, stack_ref, 0, SIDE + 2)
    back_hidden = turned_dot(windows[...], columns_ref[...])
    back_pre = back_hidden * slope
    back_conv = rounded(back_pre * gain)
    inner[RIM : 2 * RIM] = back_conv.astype(BF16)

    def own(value):
        lead = value.reshape(SIDE + 2, SIDE + 2, SIDE, LANES)
        return lead[1 : SIDE + 1, 1 : SIDE + 1].reshape(OWN, LANES)

    own_pre = own(back_pre)
    gain_term = jnp.sum(own_pre * own(first_conv), axis=0, keepdims=True)
    bias_term = jnp.sum(own_pre, axis=0, keepdims=True)

    fill_windows(windows, stack_ref, 1, SIDE)
    hidden_turned = own(hidden).T.astype(BF16)
    terms_two[...] = plain_dot(hidden_turned, windows[0:OWN])

    lead = back_conv.reshape(SIDE + 2, SIDE + 2, SIDE, LANES)
    stack_ref[0 : SIDE + 2, 0 : SIDE + 2] = with_neighbours(lead)
    fill_windows(windows, stack_ref, 0, SIDE)
    features_turned = grid[0].reshape(OWN, LANES).T.astype(BF16)
    terms_one[...] = plain_dot(features_turned, windows[0:OWN])

    lane = lax.broadcasted_iota(jnp.int32, (C, LANES), 1)
    for terms, packed in ((terms_one, packed_all.at[0]), (terms_two, packed_all.at[1])):

        def term(tap):
            at = (TAPS - 1 - tap) * LANES
            return terms[0:C, at : at + LANES]

        for group in range(6):
            split = term(4 * group + 3)
            for part in range(3):
                row = (3 * group + part) * C
                moved = pltpu.roll(split, C - 32 * part, 1)
                joined = jnp.where(lane < C, term(4 * group + part), moved)
                packed[row : row + C] = joined
        for tap in range(24, TAPS):
            packed[(tap - 6) * C : (tap - 5) * C] = term(tap)
    blank = jnp.zeros((HALF - 21 * C - 2, LANES), F32)
    packed_all[0, 21 * C : HALF] = jnp.zeros((HALF - 21 * C, LANES), F32)
    packed_all[1, 21 * C : HALF] = jnp.concatenate([gain_term, bias_term, blank], axis=0)
    keep[...] = packed_all[sides[0]]
    send[...] = packed_all[1 - sides[0]]


def output_kernel(
    slots, grid, inner, one_far, two_far, out, grad,
    stack_ref, windows, rows_ref, columns_ref, weight_one, weight_two, sems,
):
    copies = started(((one_far, weight_one), (two_far, weight_two)), sems)
    for copy in copies:
        copy.wait()
    spread(weight_two, rows_ref)
    spread_flipped(weight_one, columns_ref)
    count = out.shape[0]
    out[...] = jnp.zeros_like(out)
    grad[...] = jnp.zeros_like(grad)
    for field, target in enumerate((out, grad)):
        lead = inner[field * RIM : field * RIM + RIM].astype(F32)
        stack_ref[...] = with_neighbours(lead.reshape(SIDE + 2, SIDE + 2, SIDE, LANES))
        fill_windows(windows, stack_ref, 0, SIDE)
        if field == 0:
            total = plain_dot(windows[...], rows_ref[...])
        else:
            total = turned_dot(windows[...], columns_ref[...])
        dense = total.reshape(SIDE, SIDE, SIDE, LANES) + grid[field]
        for i in range(2):
            for j in range(2):
                column = dense[4 * i : 4 * i + 4, 4 * j : 4 * j + 4].reshape(4, 2, 2, 8, LANES)
                even = column[:, :, 0].reshape(8, 8, LANES)
                odd = column[:, :, 1].reshape(8, 8, LANES)
                is_low = sublane_low(even.shape)
                tiles = (
                    jnp.where(is_low, even, rotated(odd, 4)),
                    jnp.where(is_low, rotated(even, 4), odd),
                )
                for k in range(2):
                    slot = slots[0, 0, i, j, k]
                    brick = tiles[k].reshape(64, LANES)[:, 0:C].astype(BF16)

                    @pl.when(slot < count)
                    def _():
                        target[slot] = brick


def unpack(scale, parts, grad):
    lane = lax.broadcasted_iota(jnp.int32, (C, LANES), 1)
    for group in range(6):
        held = [
            parts[(3 * group + part) * C : (3 * group + part + 1) * C].astype(F32) * scale
            for part in range(3)
        ]
        for part in range(3):
            grad[4 * group + part] = held[part][:, 0:C]
        moved = [pltpu.roll(held[part], 32 * part + 32, 1) for part in range(3)]
        last = jnp.where(lane < 32, moved[0], jnp.where(lane < 64, moved[1], moved[2]))
        grad[4 * group + 3] = last[:, 0:C]
    for tap in range(24, TAPS):
        grad[tap] = parts[(tap - 6) * C : (tap - 5) * C].astype(F32)[:, 0:C] * scale


def finish_kernel(scale, mine, other, grad_one, grad_two, grad_gain, grad_bias, parts):
    sides = parities()
    parts[sides[0]] = mine[...]
    parts[1 - sides[0]] = other[...]
    unpack(scale, parts.at[0], grad_one)
    unpack(scale, parts.at[1], grad_two)
    rest = parts[1, 21 * C : HALF].astype(F32) * scale
    grad_gain[...] = rest[0:1, 0:C]
    grad_bias[...] = rest[1:2, 0:C]


def shape(dims, dtype):
    return jax.ShapeDtypeStruct(dims, dtype)


def dense_parts(features, cotangent, slots):
    return call(
        grid_kernel,
        (shape((2, SIDE, SIDE, SIDE, LANES), F32), shape((256, LANES), BF16), shape((256, LANES), BF16)),
        [HBM_SPEC] * 3,
        scratch=[
            pltpu.VMEM((4, 16, SIDE, LANES), F32),
            pltpu.SMEM(slots.shape, jnp.int32),
            pltpu.VMEM(features.shape, BF16),
            pltpu.VMEM(features.shape, BF16),
            pltpu.SemaphoreType.DMA((3,)),
        ],
        moved=2_000_000,
        name="dense_grid",
    )(*kept_far(slots, features, cotangent))


def rims(grid, far_x, near_x):
    return call(
        rim_kernel,
        (shape((384, LANES), BF16), shape((384, LANES), BF16)),
        [VMEM_SPEC] * 3,
        moved=1_500_000,
        name="rims",
    )(grid, far_x, near_x)


def weight_scratch():
    return [
        pltpu.VMEM((SPAN, LANES), BF16),
        pltpu.VMEM((LANES, SPAN), BF16),
        pltpu.VMEM((TAPS, C, C), BF16),
        pltpu.VMEM((TAPS, C, C), BF16),
    ]


def prepare(weight_one, weight_two, gain, bias):
    prepared = call(
        prepare_kernel,
        (shape((SPAN, LANES), BF16), shape((LANES, SPAN), BF16), shape((2, LANES), F32)),
        [HBM_SPEC] * 4,
        scratch=[
            pltpu.VMEM((TAPS, C, C), BF16),
            pltpu.VMEM((TAPS, C, C), BF16),
            pltpu.VMEM((1, C), F32),
            pltpu.VMEM((1, C), F32),
            pltpu.SemaphoreType.DMA((4,)),
        ],
        moved=3_000_000,
        name="prepare",
    )(*kept_far(weight_one, weight_two, gain.reshape(1, C), bias.reshape(1, C)))
    return [pltpu.with_memory_space_constraint(array, pltpu.VMEM) for array in prepared]


def gradients(grid, halos, rows, columns, gain_bias):
    return call(
        gradient_kernel,
        (shape((HALF, LANES), F32), shape((HALF, LANES), F32), shape((2 * RIM, LANES), BF16)),
        [VMEM_SPEC] * 8,
        scratch=[
            pltpu.VMEM((SIDE + 4, SIDE + 4, SIDE, LANES), F32),
            pltpu.VMEM((SIDE + 4, SIDE + 4, SIDE, 3 * LANES), F32),
            pltpu.VMEM((RIM, SPAN), BF16),
            pltpu.VMEM((LANES, SPAN), F32),
            pltpu.VMEM((LANES, SPAN), F32),
            pltpu.VMEM((2, HALF, LANES), F32),
        ],
        flops=2_400_000_000,
        moved=8_000_000,
        name="gradients",
        room=28,
    )(grid, *halos, rows, columns, gain_bias)


def outputs(slots, grid, inner, weight_one, weight_two):
    result = shape((4, 64, C), BF16)
    return call(
        output_kernel,
        (result, result),
        [SMEM_SPEC] + [VMEM_SPEC] * 2 + [HBM_SPEC] * 2,
        scratch=[
            pltpu.VMEM((SIDE + 2, SIDE + 2, SIDE, 3 * LANES), F32),
            pltpu.VMEM((OWN, SPAN), BF16),
            *weight_scratch(),
            pltpu.SemaphoreType.DMA((2,)),
        ],
        flops=900_000_000,
        moved=4_000_000,
        name="outputs",
        room=18,
    )(slots, grid, inner, *kept_far(weight_one, weight_two))


def finish(mine, other, scale):
    grads, line = shape((TAPS, C, C), F32), shape((1, C), F32)
    return call(
        functools.partial(finish_kernel, scale),
        (grads, grads, line, line),
        [VMEM_SPEC, VMEM_SPEC],
        scratch=[pltpu.VMEM((2, HALF, LANES), BF16)],
        moved=4_000_000,
        name="finish",
    )(mine, other)


SIZES = dict(y=4, zh=4, core=2, zl=2, zp=2, x=4)
PLANE = ("y", "x", "zp")
LINE = ("zh", "zl")


def spread_out(block, axes):
    copies = jnp.broadcast_to(block, (lax.axis_size(axes),) + block.shape)
    return lax.all_to_all(copies, axes, 0, 0)


def other_core(block):
    return lax.ppermute(block, "core", [(0, 1), (1, 0)])


def reduce_all(keep, send, beside):
    pair = (keep + other_core(send)).astype(BF16)
    parts = lax.all_to_all(pair.reshape(lax.axis_size(PLANE), -1, LANES), PLANE, 0, 0)
    chunk = jnp.sum(parts.astype(F32), axis=0)
    chunks, beside = lax.optimization_barrier((spread_out(chunk, LINE), beside))
    chunk = jnp.sum(chunks, axis=0)
    return spread_out(chunk.astype(BF16), PLANE).reshape(HALF, LANES), beside


GX = ("y", "zh", "core")
GY = ("zl", "zp", "x")


def swapped(far, near, axis):
    count = lax.axis_size(axis)
    ends = {n: n + 1 for n in range(1, count - 1, 2)}
    route = [pair for low, high in ends.items() for pair in ((low, high), (high, low))]
    far = lax.ppermute(far, axis, route)
    near = lax.ppermute(near, axis, [(n, n ^ 1) for n in range(count)])
    return far, near


def body(features, cotangent, brick_slot, weight_one, weight_two, gain, bias):
    grid, far, near = dense_parts(features, cotangent, brick_slot)
    far, near, *given = lax.optimization_barrier((far, near, weight_one, weight_two, gain, bias))
    around_x = swapped(far, near, GX)
    around_x, prepared = lax.optimization_barrier((around_x, prepare(*given)))
    far, near = rims(grid, *around_x)
    halos = (*around_x, *swapped(far, near, GY))
    keep, send, inner = gradients(grid, halos, *prepared)
    out, grad = outputs(brick_slot, grid, inner, weight_one, weight_two)
    out, grad = out.reshape(features.shape), grad.reshape(features.shape)
    mine, (out, grad) = reduce_all(keep, send, (out, grad))
    other = other_core(mine)
    scale = 1.0 / math.sqrt(lax.axis_size(GX) * lax.axis_size(GY) * 256)
    grad_one, grad_two, grad_gain, grad_bias = finish(mine, other, scale)
    return (
        out,
        grad,
        grad_one,
        grad_two,
        grad_gain.reshape(gain.shape),
        grad_bias.reshape(bias.shape),
    )


def solution(mesh):
    fine = jax.sharding.Mesh(mesh.devices.reshape(tuple(SIZES.values())), tuple(SIZES))
    slabs = P(GX, GY, None, None)
    in_specs = (slabs, slabs, P(GX, GY, None, None, None), P(), P(), P(), P())
    out_specs = (slabs, slabs, P(), P(), P(), P())
    return jax.shard_map(body, mesh=fine, in_specs=in_specs, out_specs=out_specs, check_vma=False)
```

```python
import functools
import math

import jax
import jax.numpy as jnp
from jax import lax
from jax.experimental import pallas as pl
from jax.experimental.pallas import tpu as pltpu
from jax.sharding import PartitionSpec as P

C = 96
LANES = 128
SIDE = 8
TAPS = 27
SPAN = TAPS * LANES
OWN = 512
RIM = 800
HALF = 2048
F32 = jnp.float32
BF16 = jnp.bfloat16

VMEM_SPEC = pl.BlockSpec(memory_space=pltpu.VMEM)
SMEM_SPEC = pl.BlockSpec(memory_space=pltpu.SMEM)
HBM_SPEC = pl.BlockSpec(memory_space=pltpu.HBM)


def call(kernel, out_shape, specs, scratch=(), flops=0, moved=0, name=None, room=8):
    return pl.pallas_call(
        kernel,
        out_shape=out_shape,
        in_specs=specs,
        out_specs=jax.tree.map(lambda _: VMEM_SPEC, out_shape),
        scratch_shapes=list(scratch),
        cost_estimate=pl.CostEstimate(flops=flops, bytes_accessed=moved, transcendentals=0),
        name=name,
        compiler_params=pltpu.CompilerParams(vmem_limit_bytes=room << 20),
    )


def sublane_low(shape):
    return lax.broadcasted_iota(jnp.int32, shape, len(shape) - 2) < 4


def rotated(value, shift):
    flat = value.reshape((-1,) + value.shape[-2:])
    return pltpu.roll(flat, shift, 1).reshape(value.shape)


def kept_far(*arrays):
    return [pltpu.with_memory_space_constraint(array, pltpu.HBM) for array in arrays]


def started(pairs, sems):
    copies = [pltpu.make_async_copy(*pair, sems.at[n]) for n, pair in enumerate(pairs)]
    for copy in copies:
        copy.start()
    return copies


def grid_kernel(
    slots_far, features_far, cotangent_far, grid, far, near,
    lines, slots, features, cotangent, sems,
):
    copies = started(
        ((features_far, features), (cotangent_far, cotangent), (slots_far, slots)), sems
    )
    copies[2].wait()
    sides = parities()
    lane = lax.broadcasted_iota(jnp.int32, (16, 4, LANES), 2)
    spot = lax.broadcasted_iota(jnp.int32, (16, SIDE, LANES), 1)
    for field, source in enumerate((features, cotangent)):
        copies[field].wait()
        whole = source[0, 0].astype(F32)

        def tiles(part):
            starts = [(3 * line + part) * LANES for line in range(16)]
            return jnp.stack([whole[:, at : at + LANES] for at in starts], axis=0)

        first, middle, last = tiles(0), tiles(1), tiles(2)
        voxels = (
            first,
            jnp.where(lane < 32, moved_lanes(first, 32), moved_lanes(middle, 32)),
            jnp.where(lane < 64, moved_lanes(middle, 64), moved_lanes(last, 64)),
            moved_lanes(last, 96),
        )
        for w in range(4):
            lines[w] = jnp.zeros((16, SIDE, LANES), F32)
            lines[w, :, 0:4] = jnp.where(lane < C, voxels[w], 1.0 - field)
        for i in range(2):
            for j in range(2):
                tile = None
                for z in range(SIDE):
                    row = lines[z % 4, :, pl.ds(slots[0, 0, i, j, z // 4], 1)]
                    row = jnp.broadcast_to(row, (16, SIDE, LANES))
                    tile = row if tile is None else jnp.where(spot == z, row, tile)
                grid[field, 4 * i : 4 * i + 4, 4 * j : 4 * j + 4] = tile.reshape(4, 4, SIDE, LANES)
    for field in range(2):
        rows = slice(field * 128, field * 128 + 128)
        for message, at in ((near, 6 - 6 * sides[0]), (far, 6 * sides[0])):
            message[rows] = grid[field, pl.ds(at, 2)].reshape(128, LANES).astype(BF16)


def moved_lanes(value, shift):
    return pltpu.roll(value.reshape(64, LANES), shift, 1).reshape(16, 4, LANES)


def parities():
    return lax.axis_index("core"), lax.axis_index("x") & 1


def opened(message, lead):
    return message.astype(F32).reshape(lead + (SIDE, LANES))


def lower_upper(side, near, far, lead):
    near, far = opened(near[...], lead), opened(far[...], lead)
    even = side == 0
    return jnp.where(even, far, near), jnp.where(even, near, far)


def rim_kernel(grid, far_x, near_x, far, near):
    sides = parities()
    lower, upper = lower_upper(sides[0], near_x, far_x, (2, 2, SIDE))
    even = sides[1] == 0

    def picked(block, message):
        first, last = block[:, 0:2], block[:, SIDE - 2 : SIDE]
        chosen = jnp.where(even, last, first) if message is near else jnp.where(even, first, last)
        return chosen.reshape(32, LANES).astype(BF16)

    for message, at in ((near, 6 - 6 * sides[1]), (far, 6 * sides[1])):
        for field in range(2):
            base = field * 192
            message[base : base + 32] = picked(lower[field], message)
            own = grid[field, :, pl.ds(at, 2)].reshape(128, LANES)
            message[base + 32 : base + 160] = own.astype(BF16)
            message[base + 160 : base + 192] = picked(upper[field], message)


def with_neighbours(value):
    spot = lax.broadcasted_iota(jnp.int32, value.shape, value.ndim - 2)
    before = jnp.where(spot == 0, 0.0, rotated(value, 1))
    after = jnp.where(spot == SIDE - 1, 0.0, rotated(value, SIDE - 1))
    return jnp.concatenate([before, value, after], axis=value.ndim - 1)


def fill_windows(windows, stacked, start, extent):
    rows = extent * extent * SIDE
    for wx in range(3):
        for wy in range(3):
            at = (wx * 3 + wy) * 3 * LANES
            piece = stacked[
                start + wx : start + wx + extent, start + wy : start + wy + extent
            ]
            windows[0:rows, at : at + 3 * LANES] = piece.reshape(rows, 3 * LANES).astype(BF16)


def spread(kernel, rows_ref):
    rows_ref[...] = jnp.zeros_like(rows_ref)
    for tap in range(TAPS):
        rows_ref[tap * LANES : tap * LANES + C, 0:C] = kernel[tap]


def spread_flipped(kernel, columns_ref):
    columns_ref[...] = jnp.zeros_like(columns_ref)
    for tap in range(TAPS):
        columns_ref[0:C, tap * LANES : tap * LANES + C] = kernel[TAPS - 1 - tap]


def prepare_kernel(
    one_far, two_far, gain_far, bias_far, rows_ref, columns_ref, gain_bias,
    weight_one, weight_two, gain_ref, bias_ref, sems,
):
    copies = started(
        ((one_far, weight_one), (two_far, weight_two), (gain_far, gain_ref), (bias_far, bias_ref)), sems
    )
    for copy in copies:
        copy.wait()
    spread(weight_one, rows_ref)
    spread_flipped(weight_two, columns_ref)
    gain_bias[...] = jnp.zeros_like(gain_bias)
    gain_bias[0:1, 0:C] = gain_ref[...]
    gain_bias[1:2, 0:C] = bias_ref[...]


def plain_dot(left, right):
    return jnp.dot(left, right, preferred_element_type=F32)


def turned_dot(left, right):
    return lax.dot_general(left, right, (((1,), (1,)), ((), ())), preferred_element_type=F32)


def rounded(value):
    return value.astype(BF16).astype(F32)


def gradient_kernel(
    grid, far_x, near_x, far_y, near_y, rows_ref, columns_ref, gain_bias,
    keep, send, inner,
    field_ref, stack_ref, windows, terms_one, terms_two, packed_all,
):
    sides = parities()
    gain, bias = gain_bias[0:1], gain_bias[1:2]
    lower, upper = lower_upper(sides[0], near_x, far_x, (2, 2, SIDE))
    to_left, to_right = lower_upper(sides[1], near_y, far_y, (2, SIDE + 4, 2))

    def load_field(field):
        field_ref[2 : SIDE + 2, 2 : SIDE + 2] = grid[field]
        field_ref[0:2, 2 : SIDE + 2] = lower[field]
        field_ref[SIDE + 2 : SIDE + 4, 2 : SIDE + 2] = upper[field]
        field_ref[:, 0:2] = to_left[field]
        field_ref[:, SIDE + 2 : SIDE + 4] = to_right[field]

    load_field(0)
    mark = field_ref[1 : SIDE + 3, 1 : SIDE + 3].reshape(RIM, LANES)[:, C : C + 1]
    stack_ref[...] = with_neighbours(field_ref[...])
    fill_windows(windows, stack_ref, 0, SIDE + 2)
    first_conv = plain_dot(windows[...], rows_ref[...]) * mark
    pre = first_conv * gain + bias
    gate = 1.0 / (1.0 + jnp.exp(-pre))
    hidden = rounded(pre * gate * mark)
    slope = gate * (1.0 + pre * (1.0 - gate)) * mark
    inner[0:RIM] = hidden.astype(BF16)

    load_field(1)
    stack_ref[...] = with_neighbours(field_ref[...])
    fill_windows(windows, stack_ref, 0, SIDE + 2)
    back_hidden = turned_dot(windows[...], columns_ref[...])
    back_pre = back_hidden * slope
    back_conv = rounded(back_pre * gain)
    inner[RIM : 2 * RIM] = back_conv.astype(BF16)

    def own(value):
        lead = value.reshape(SIDE + 2, SIDE + 2, SIDE, LANES)
        return lead[1 : SIDE + 1, 1 : SIDE + 1].reshape(OWN, LANES)

    own_pre = own(back_pre)
    gain_term = jnp.sum(own_pre * own(first_conv), axis=0, keepdims=True)
    bias_term = jnp.sum(own_pre, axis=0, keepdims=True)

    fill_windows(windows, stack_ref, 1, SIDE)
    hidden_turned = own(hidden).T.astype(BF16)
    terms_two[...] = plain_dot(hidden_turned, windows[0:OWN])

    lead = back_conv.reshape(SIDE + 2, SIDE + 2, SIDE, LANES)
    stack_ref[0 : SIDE + 2, 0 : SIDE + 2] = with_neighbours(lead)
    fill_windows(windows, stack_ref, 0, SIDE)
    features_turned = grid[0].reshape(OWN, LANES).T.astype(BF16)
    terms_one[...] = plain_dot(features_turned, windows[0:OWN])

    lane = lax.broadcasted_iota(jnp.int32, (C, LANES), 1)
    for terms, packed in ((terms_one, packed_all.at[0]), (terms_two, packed_all.at[1])):

        def term(tap):
            at = (TAPS - 1 - tap) * LANES
            return terms[0:C, at : at + LANES]

        for group in range(6):
            split = term(4 * group + 3)
            for part in range(3):
                row = (3 * group + part) * C
                moved = pltpu.roll(split, C - 32 * part, 1)
                joined = jnp.where(lane < C, term(4 * group + part), moved)
                packed[row : row + C] = joined
        for tap in range(24, TAPS):
            packed[(tap - 6) * C : (tap - 5) * C] = term(tap)
    blank = jnp.zeros((HALF - 21 * C - 2, LANES), F32)
    packed_all[0, 21 * C : HALF] = jnp.zeros((HALF - 21 * C, LANES), F32)
    packed_all[1, 21 * C : HALF] = jnp.concatenate([gain_term, bias_term, blank], axis=0)
    keep[...] = packed_all[sides[0]]
    send[...] = packed_all[1 - sides[0]]


def output_kernel(
    slots, grid, inner, one_far, two_far, out, grad,
    stack_ref, windows, rows_ref, columns_ref, weight_one, weight_two, sems,
):
    copies = started(((one_far, weight_one), (two_far, weight_two)), sems)
    for copy in copies:
        copy.wait()
    spread(weight_two, rows_ref)
    spread_flipped(weight_one, columns_ref)
    count = out.shape[0]
    out[...] = jnp.zeros_like(out)
    grad[...] = jnp.zeros_like(grad)
    for field, target in enumerate((out, grad)):
        lead = inner[field * RIM : field * RIM + RIM].astype(F32)
        stack_ref[...] = with_neighbours(lead.reshape(SIDE + 2, SIDE + 2, SIDE, LANES))
        fill_windows(windows, stack_ref, 0, SIDE)
        if field == 0:
            total = plain_dot(windows[...], rows_ref[...])
        else:
            total = turned_dot(windows[...], columns_ref[...])
        dense = total.reshape(SIDE, SIDE, SIDE, LANES) + grid[field]
        for i in range(2):
            for j in range(2):
                column = dense[4 * i : 4 * i + 4, 4 * j : 4 * j + 4].reshape(4, 2, 2, 8, LANES)
                even = column[:, :, 0].reshape(8, 8, LANES)
                odd = column[:, :, 1].reshape(8, 8, LANES)
                is_low = sublane_low(even.shape)
                tiles = (
                    jnp.where(is_low, even, rotated(odd, 4)),
                    jnp.where(is_low, rotated(even, 4), odd),
                )
                for k in range(2):
                    slot = slots[0, 0, i, j, k]
                    brick = tiles[k].reshape(64, LANES)[:, 0:C].astype(BF16)

                    @pl.when(slot < count)
                    def _():
                        target[slot] = brick


def unpack(scale, parts, grad):
    lane = lax.broadcasted_iota(jnp.int32, (C, LANES), 1)
    for group in range(6):
        held = [
            parts[(3 * group + part) * C : (3 * group + part + 1) * C].astype(F32) * scale
            for part in range(3)
        ]
        for part in range(3):
            grad[4 * group + part] = held[part][:, 0:C]
        moved = [pltpu.roll(held[part], 32 * part + 32, 1) for part in range(3)]
        last = jnp.where(lane < 32, moved[0], jnp.where(lane < 64, moved[1], moved[2]))
        grad[4 * group + 3] = last[:, 0:C]
    for tap in range(24, TAPS):
        grad[tap] = parts[(tap - 6) * C : (tap - 5) * C].astype(F32)[:, 0:C] * scale


def put(held, first, grads, sem):
    for place in range(2):

        @pl.when(first == place)
        def _():
            copy = pltpu.make_async_copy(held, grads[place], sem)
            copy.start()
            copy.wait()


def half_kernel(scale, parts, grad_one, grad_two, held, sem):
    unpack(scale, parts, held)
    put(held, parities()[0], (grad_one, grad_two), sem)


def finish_kernel(
    scale, one_in, two_in, mine, other, grad_one, grad_two, grad_gain, grad_bias, held, sem
):
    core = parities()[0]
    unpack(scale, other, held)
    put(held, core, (grad_two, grad_one), sem)
    last = slice(21 * C, HALF)
    rest = jnp.where(core == 1, mine[last].astype(F32), other[last].astype(F32)) * scale
    grad_gain[...] = rest[0:1, 0:C]
    grad_bias[...] = rest[1:2, 0:C]


def shape(dims, dtype):
    return jax.ShapeDtypeStruct(dims, dtype)


def dense_parts(features, cotangent, slots):
    return call(
        grid_kernel,
        (shape((2, SIDE, SIDE, SIDE, LANES), F32), shape((256, LANES), BF16), shape((256, LANES), BF16)),
        [HBM_SPEC] * 3,
        scratch=[
            pltpu.VMEM((4, 16, SIDE, LANES), F32),
            pltpu.SMEM(slots.shape, jnp.int32),
            pltpu.VMEM(features.shape, BF16),
            pltpu.VMEM(features.shape, BF16),
            pltpu.SemaphoreType.DMA((3,)),
        ],
        moved=2_000_000,
        name="dense_grid",
    )(*kept_far(slots, features, cotangent))


def rims(grid, far_x, near_x):
    return call(
        rim_kernel,
        (shape((384, LANES), BF16), shape((384, LANES), BF16)),
        [VMEM_SPEC] * 3,
        moved=1_500_000,
        name="rims",
    )(grid, far_x, near_x)


def weight_scratch():
    return [
        pltpu.VMEM((SPAN, LANES), BF16),
        pltpu.VMEM((LANES, SPAN), BF16),
        pltpu.VMEM((TAPS, C, C), BF16),
        pltpu.VMEM((TAPS, C, C), BF16),
    ]


def prepare(weight_one, weight_two, gain, bias):
    prepared = call(
        prepare_kernel,
        (shape((SPAN, LANES), BF16), shape((LANES, SPAN), BF16), shape((2, LANES), F32)),
        [HBM_SPEC] * 4,
        scratch=[
            pltpu.VMEM((TAPS, C, C), BF16),
            pltpu.VMEM((TAPS, C, C), BF16),
            pltpu.VMEM((1, C), F32),
            pltpu.VMEM((1, C), F32),
            pltpu.SemaphoreType.DMA((4,)),
        ],
        moved=3_000_000,
        name="prepare",
    )(*kept_far(weight_one, weight_two, gain.reshape(1, C), bias.reshape(1, C)))
    return [pltpu.with_memory_space_constraint(array, pltpu.VMEM) for array in prepared]


def gradients(grid, halos, rows, columns, gain_bias):
    return call(
        gradient_kernel,
        (shape((HALF, LANES), F32), shape((HALF, LANES), F32), shape((2 * RIM, LANES), BF16)),
        [VMEM_SPEC] * 8,
        scratch=[
            pltpu.VMEM((SIDE + 4, SIDE + 4, SIDE, LANES), F32),
            pltpu.VMEM((SIDE + 4, SIDE + 4, SIDE, 3 * LANES), F32),
            pltpu.VMEM((RIM, SPAN), BF16),
            pltpu.VMEM((LANES, SPAN), F32),
            pltpu.VMEM((LANES, SPAN), F32),
            pltpu.VMEM((2, HALF, LANES), F32),
        ],
        flops=2_400_000_000,
        moved=8_000_000,
        name="gradients",
        room=28,
    )(grid, *halos, rows, columns, gain_bias)


def outputs(slots, grid, inner, weight_one, weight_two):
    result = shape((4, 64, C), BF16)
    return call(
        output_kernel,
        (result, result),
        [SMEM_SPEC] + [VMEM_SPEC] * 2 + [HBM_SPEC] * 2,
        scratch=[
            pltpu.VMEM((SIDE + 2, SIDE + 2, SIDE, 3 * LANES), F32),
            pltpu.VMEM((OWN, SPAN), BF16),
            *weight_scratch(),
            pltpu.SemaphoreType.DMA((2,)),
        ],
        flops=900_000_000,
        moved=4_000_000,
        name="outputs",
        room=18,
    )(slots, grid, inner, *kept_far(weight_one, weight_two))


FAR_OUT = pl.BlockSpec(memory_space=pltpu.HBM)


def half_finished(mine, scale):
    grads = shape((TAPS, C, C), F32)
    return pl.pallas_call(
        functools.partial(half_kernel, scale),
        out_shape=(grads, grads),
        in_specs=[VMEM_SPEC],
        out_specs=(FAR_OUT, FAR_OUT),
        scratch_shapes=[pltpu.VMEM((TAPS, C, C), F32), pltpu.SemaphoreType.DMA],
        cost_estimate=pl.CostEstimate(flops=0, bytes_accessed=3_000_000, transcendentals=0),
        compiler_params=pltpu.CompilerParams(vmem_limit_bytes=8 << 20),
        name="half_finish",
    )(mine)


def finish(halves, mine, other, scale):
    grads, line = shape((TAPS, C, C), F32), shape((1, C), F32)
    return pl.pallas_call(
        functools.partial(finish_kernel, scale),
        out_shape=(grads, grads, line, line),
        in_specs=[HBM_SPEC, HBM_SPEC, VMEM_SPEC, VMEM_SPEC],
        out_specs=(FAR_OUT, FAR_OUT, VMEM_SPEC, VMEM_SPEC),
        scratch_shapes=[pltpu.VMEM((TAPS, C, C), F32), pltpu.SemaphoreType.DMA],
        input_output_aliases={0: 0, 1: 1},
        cost_estimate=pl.CostEstimate(flops=0, bytes_accessed=3_000_000, transcendentals=0),
        compiler_params=pltpu.CompilerParams(vmem_limit_bytes=8 << 20),
        name="finish",
    )(*halves, mine, other)


SIZES = dict(y=4, zh=4, core=2, zl=2, zp=2, x=4)
PLANE = ("y", "x", "zp")
LINE = ("zh", "zl")


def spread_out(block, axes):
    copies = jnp.broadcast_to(block, (lax.axis_size(axes),) + block.shape)
    return lax.all_to_all(copies, axes, 0, 0)


def other_core(block):
    return lax.ppermute(block, "core", [(0, 1), (1, 0)])


def reduce_all(keep, send, beside):
    pair = (keep + other_core(send)).astype(BF16)
    parts = lax.all_to_all(pair.reshape(lax.axis_size(PLANE), -1, LANES), PLANE, 0, 0)
    chunk = jnp.sum(parts.astype(F32), axis=0)
    chunks, beside = lax.optimization_barrier((spread_out(chunk, LINE), beside))
    chunk = jnp.sum(chunks, axis=0)
    return spread_out(chunk.astype(BF16), PLANE).reshape(HALF, LANES), beside


GX = ("y", "zh", "core")
GY = ("zl", "zp", "x")


def swapped(far, near, axis):
    count = lax.axis_size(axis)
    ends = {n: n + 1 for n in range(1, count - 1, 2)}
    route = [pair for low, high in ends.items() for pair in ((low, high), (high, low))]
    far = lax.ppermute(far, axis, route)
    near = lax.ppermute(near, axis, [(n, n ^ 1) for n in range(count)])
    return far, near


def body(features, cotangent, brick_slot, weight_one, weight_two, gain, bias):
    grid, far, near = dense_parts(features, cotangent, brick_slot)
    far, near, *given = lax.optimization_barrier((far, near, weight_one, weight_two, gain, bias))
    around_x = swapped(far, near, GX)
    around_x, prepared = lax.optimization_barrier((around_x, prepare(*given)))
    far, near = rims(grid, *around_x)
    halos = (*around_x, *swapped(far, near, GY))
    keep, send, inner = gradients(grid, halos, *prepared)
    out, grad = outputs(brick_slot, grid, inner, weight_one, weight_two)
    out, grad = out.reshape(features.shape), grad.reshape(features.shape)
    mine, (out, grad) = reduce_all(keep, send, (out, grad))
    other = other_core(mine)
    scale = 1.0 / math.sqrt(lax.axis_size(GX) * lax.axis_size(GY) * 256)
    halves = half_finished(mine, scale)
    grad_one, grad_two, grad_gain, grad_bias = finish(halves, mine, other, scale)
    return (
        out,
        grad,
        grad_one,
        grad_two,
        grad_gain.reshape(gain.shape),
        grad_bias.reshape(bias.shape),
    )


def solution(mesh):
    fine = jax.sharding.Mesh(mesh.devices.reshape(tuple(SIZES.values())), tuple(SIZES))
    slabs = P(GX, GY, None, None)
    in_specs = (slabs, slabs, P(GX, GY, None, None, None), P(), P(), P(), P())
    out_specs = (slabs, slabs, P(), P(), P(), P())
    return jax.shard_map(body, mesh=fine, in_specs=in_specs, out_specs=out_specs, check_vma=False)
```

```python
import functools
import math

import jax
import jax.numpy as jnp
from jax import lax
from jax.experimental import pallas as pl
from jax.experimental.pallas import tpu as pltpu
from jax.sharding import PartitionSpec as P

C = 96
LANES = 128
SIDE = 8
TAPS = 27
SPAN = TAPS * LANES
OWN = 512
RIM = 800
HALF = 2048
F32 = jnp.float32
BF16 = jnp.bfloat16

VMEM_SPEC = pl.BlockSpec(memory_space=pltpu.VMEM)
SMEM_SPEC = pl.BlockSpec(memory_space=pltpu.SMEM)
HBM_SPEC = pl.BlockSpec(memory_space=pltpu.HBM)


def call(kernel, out_shape, specs, scratch=(), flops=0, moved=0, name=None, room=8):
    return pl.pallas_call(
        kernel,
        out_shape=out_shape,
        in_specs=specs,
        out_specs=jax.tree.map(lambda _: VMEM_SPEC, out_shape),
        scratch_shapes=list(scratch),
        cost_estimate=pl.CostEstimate(flops=flops, bytes_accessed=moved, transcendentals=0),
        name=name,
        compiler_params=pltpu.CompilerParams(vmem_limit_bytes=room << 20),
    )


def sublane_low(shape):
    return lax.broadcasted_iota(jnp.int32, shape, len(shape) - 2) < 4


def rotated(value, shift):
    flat = value.reshape((-1,) + value.shape[-2:])
    return pltpu.roll(flat, shift, 1).reshape(value.shape)


def kept_far(*arrays):
    return [pltpu.with_memory_space_constraint(array, pltpu.HBM) for array in arrays]


def started(pairs, sems):
    copies = [pltpu.make_async_copy(*pair, sems.at[n]) for n, pair in enumerate(pairs)]
    for copy in copies:
        copy.start()
    return copies


def grid_kernel(
    slots_far, features_far, cotangent_far, grid, far, near,
    lines, slots, features, cotangent, sems,
):
    copies = started(
        ((features_far, features), (cotangent_far, cotangent), (slots_far, slots)), sems
    )
    copies[2].wait()
    sides = parities()
    lane = lax.broadcasted_iota(jnp.int32, (16, 4, LANES), 2)
    spot = lax.broadcasted_iota(jnp.int32, (16, SIDE, LANES), 1)
    for field, source in enumerate((features, cotangent)):
        copies[field].wait()
        whole = source[0, 0].astype(F32)

        def tiles(part):
            starts = [(3 * line + part) * LANES for line in range(16)]
            return jnp.stack([whole[:, at : at + LANES] for at in starts], axis=0)

        first, middle, last = tiles(0), tiles(1), tiles(2)
        voxels = (
            first,
            jnp.where(lane < 32, moved_lanes(first, 32), moved_lanes(middle, 32)),
            jnp.where(lane < 64, moved_lanes(middle, 64), moved_lanes(last, 64)),
            moved_lanes(last, 96),
        )
        for w in range(4):
            lines[w] = jnp.zeros((16, SIDE, LANES), F32)
            lines[w, :, 0:4] = jnp.where(lane < C, voxels[w], 1.0 - field)
        for i in range(2):
            for j in range(2):
                tile = None
                for z in range(SIDE):
                    row = lines[z % 4, :, pl.ds(slots[0, 0, i, j, z // 4], 1)]
                    row = jnp.broadcast_to(row, (16, SIDE, LANES))
                    tile = row if tile is None else jnp.where(spot == z, row, tile)
                grid[field, 4 * i : 4 * i + 4, 4 * j : 4 * j + 4] = tile.reshape(4, 4, SIDE, LANES)
    for field in range(2):
        rows = slice(field * 128, field * 128 + 128)
        for message, at in ((near, 6 - 6 * sides[0]), (far, 6 * sides[0])):
            message[rows] = grid[field, pl.ds(at, 2)].reshape(128, LANES).astype(BF16)


def moved_lanes(value, shift):
    return pltpu.roll(value.reshape(64, LANES), shift, 1).reshape(16, 4, LANES)


def parities():
    return lax.axis_index("core"), lax.axis_index("x") & 1


def opened(message, lead):
    return message.astype(F32).reshape(lead + (SIDE, LANES))


def lower_upper(side, near, far, lead):
    near, far = opened(near[...], lead), opened(far[...], lead)
    even = side == 0
    return jnp.where(even, far, near), jnp.where(even, near, far)


def rim_kernel(grid, far_x, near_x, far, near):
    sides = parities()
    lower, upper = lower_upper(sides[0], near_x, far_x, (2, 2, SIDE))
    even = sides[1] == 0

    def picked(block, message):
        first, last = block[:, 0:2], block[:, SIDE - 2 : SIDE]
        chosen = jnp.where(even, last, first) if message is near else jnp.where(even, first, last)
        return chosen.reshape(32, LANES).astype(BF16)

    for message, at in ((near, 6 - 6 * sides[1]), (far, 6 * sides[1])):
        for field in range(2):
            base = field * 192
            message[base : base + 32] = picked(lower[field], message)
            own = grid[field, :, pl.ds(at, 2)].reshape(128, LANES)
            message[base + 32 : base + 160] = own.astype(BF16)
            message[base + 160 : base + 192] = picked(upper[field], message)


def with_neighbours(value):
    spot = lax.broadcasted_iota(jnp.int32, value.shape, value.ndim - 2)
    before = jnp.where(spot == 0, 0.0, rotated(value, 1))
    after = jnp.where(spot == SIDE - 1, 0.0, rotated(value, SIDE - 1))
    return jnp.concatenate([before, value, after], axis=value.ndim - 1)


def fill_windows(windows, stacked, start, extent):
    rows = extent * extent * SIDE
    for wx in range(3):
        for wy in range(3):
            at = (wx * 3 + wy) * 3 * LANES
            piece = stacked[
                start + wx : start + wx + extent, start + wy : start + wy + extent
            ]
            windows[0:rows, at : at + 3 * LANES] = piece.reshape(rows, 3 * LANES).astype(BF16)


def spread(kernel, rows_ref):
    rows_ref[...] = jnp.zeros_like(rows_ref)
    for tap in range(TAPS):
        rows_ref[tap * LANES : tap * LANES + C, 0:C] = kernel[tap]


def spread_flipped(kernel, columns_ref):
    columns_ref[...] = jnp.zeros_like(columns_ref)
    for tap in range(TAPS):
        columns_ref[0:C, tap * LANES : tap * LANES + C] = kernel[TAPS - 1 - tap]


def prepare_kernel(
    one_far, two_far, gain_far, bias_far, rows_ref, columns_ref, gain_bias,
    weight_one, weight_two, gain_ref, bias_ref, sems,
):
    copies = started(
        ((one_far, weight_one), (two_far, weight_two), (gain_far, gain_ref), (bias_far, bias_ref)), sems
    )
    for copy in copies:
        copy.wait()
    spread(weight_one, rows_ref)
    spread_flipped(weight_two, columns_ref)
    gain_bias[...] = jnp.zeros_like(gain_bias)
    gain_bias[0:1, 0:C] = gain_ref[...]
    gain_bias[1:2, 0:C] = bias_ref[...]


def plain_dot(left, right):
    return jnp.dot(left, right, preferred_element_type=F32)


def turned_dot(left, right):
    return lax.dot_general(left, right, (((1,), (1,)), ((), ())), preferred_element_type=F32)


def rounded(value):
    return value.astype(BF16).astype(F32)


def gradient_kernel(
    grid, far_x, near_x, far_y, near_y, rows_ref, columns_ref, gain_bias,
    keep, send, inner,
    field_ref, stack_ref, windows, terms_one, terms_two, packed_all,
):
    sides = parities()
    gain, bias = gain_bias[0:1], gain_bias[1:2]
    lower, upper = lower_upper(sides[0], near_x, far_x, (2, 2, SIDE))
    to_left, to_right = lower_upper(sides[1], near_y, far_y, (2, SIDE + 4, 2))

    def load_field(field):
        field_ref[2 : SIDE + 2, 2 : SIDE + 2] = grid[field]
        field_ref[0:2, 2 : SIDE + 2] = lower[field]
        field_ref[SIDE + 2 : SIDE + 4, 2 : SIDE + 2] = upper[field]
        field_ref[:, 0:2] = to_left[field]
        field_ref[:, SIDE + 2 : SIDE + 4] = to_right[field]

    load_field(0)
    mark = field_ref[1 : SIDE + 3, 1 : SIDE + 3].reshape(RIM, LANES)[:, C : C + 1]
    stack_ref[...] = with_neighbours(field_ref[...])
    fill_windows(windows, stack_ref, 0, SIDE + 2)
    first_conv = plain_dot(windows[...], rows_ref[...]) * mark
    pre = first_conv * gain + bias
    gate = 1.0 / (1.0 + jnp.exp(-pre))
    hidden = rounded(pre * gate * mark)
    slope = gate * (1.0 + pre * (1.0 - gate)) * mark
    inner[0:RIM] = hidden.astype(BF16)

    load_field(1)
    stack_ref[...] = with_neighbours(field_ref[...])
    fill_windows(windows, stack_ref, 0, SIDE + 2)
    back_hidden = turned_dot(windows[...], columns_ref[...])
    back_pre = back_hidden * slope
    back_conv = rounded(back_pre * gain)
    inner[RIM : 2 * RIM] = back_conv.astype(BF16)

    def own(value):
        lead = value.reshape(SIDE + 2, SIDE + 2, SIDE, LANES)
        return lead[1 : SIDE + 1, 1 : SIDE + 1].reshape(OWN, LANES)

    own_pre = own(back_pre)
    gain_term = jnp.sum(own_pre * own(first_conv), axis=0, keepdims=True)
    bias_term = jnp.sum(own_pre, axis=0, keepdims=True)

    fill_windows(windows, stack_ref, 1, SIDE)
    hidden_turned = own(hidden).T.astype(BF16)
    terms_two[...] = plain_dot(hidden_turned, windows[0:OWN])

    lead = back_conv.reshape(SIDE + 2, SIDE + 2, SIDE, LANES)
    stack_ref[0 : SIDE + 2, 0 : SIDE + 2] = with_neighbours(lead)
    fill_windows(windows, stack_ref, 0, SIDE)
    features_turned = grid[0].reshape(OWN, LANES).T.astype(BF16)
    terms_one[...] = plain_dot(features_turned, windows[0:OWN])

    lane = lax.broadcasted_iota(jnp.int32, (C, LANES), 1)
    for terms, packed in ((terms_one, packed_all.at[0]), (terms_two, packed_all.at[1])):

        def term(tap):
            at = (TAPS - 1 - tap) * LANES
            return terms[0:C, at : at + LANES]

        for group in range(6):
            split = term(4 * group + 3)
            for part in range(3):
                row = (3 * group + part) * C
                moved = pltpu.roll(split, C - 32 * part, 1)
                joined = jnp.where(lane < C, term(4 * group + part), moved)
                packed[row : row + C] = joined
        for tap in range(24, TAPS):
            packed[(tap - 6) * C : (tap - 5) * C] = term(tap)
    blank = jnp.zeros((HALF - 21 * C - 2, LANES), F32)
    packed_all[0, 21 * C : HALF] = jnp.zeros((HALF - 21 * C, LANES), F32)
    packed_all[1, 21 * C : HALF] = jnp.concatenate([gain_term, bias_term, blank], axis=0)
    keep[...] = packed_all[sides[0]]
    send[...] = packed_all[1 - sides[0]]


def output_kernel(
    slots, grid, inner, one_far, two_far, out, grad,
    stack_ref, windows, rows_ref, columns_ref, weight_one, weight_two, sems,
):
    copies = started(((one_far, weight_one), (two_far, weight_two)), sems)
    for copy in copies:
        copy.wait()
    spread(weight_two, rows_ref)
    spread_flipped(weight_one, columns_ref)
    count = out.shape[0]
    out[...] = jnp.zeros_like(out)
    grad[...] = jnp.zeros_like(grad)
    for field, target in enumerate((out, grad)):
        lead = inner[field * RIM : field * RIM + RIM].astype(F32)
        stack_ref[...] = with_neighbours(lead.reshape(SIDE + 2, SIDE + 2, SIDE, LANES))
        fill_windows(windows, stack_ref, 0, SIDE)
        if field == 0:
            total = plain_dot(windows[...], rows_ref[...])
        else:
            total = turned_dot(windows[...], columns_ref[...])
        dense = total.reshape(SIDE, SIDE, SIDE, LANES) + grid[field]
        for i in range(2):
            for j in range(2):
                column = dense[4 * i : 4 * i + 4, 4 * j : 4 * j + 4].reshape(4, 2, 2, 8, LANES)
                even = column[:, :, 0].reshape(8, 8, LANES)
                odd = column[:, :, 1].reshape(8, 8, LANES)
                is_low = sublane_low(even.shape)
                tiles = (
                    jnp.where(is_low, even, rotated(odd, 4)),
                    jnp.where(is_low, rotated(even, 4), odd),
                )
                for k in range(2):
                    slot = slots[0, 0, i, j, k]
                    brick = tiles[k].reshape(64, LANES)[:, 0:C].astype(BF16)

                    @pl.when(slot < count)
                    def _():
                        target[slot] = brick


def unpack(scale, parts, grad, ready):
    lane = lax.broadcasted_iota(jnp.int32, (C, LANES), 1)
    for group in range(6):
        held = [
            parts[(3 * group + part) * C : (3 * group + part + 1) * C].astype(F32) * scale
            for part in range(3)
        ]
        for part in range(3):
            grad[4 * group + part] = held[part][:, 0:C]
        moved = [pltpu.roll(held[part], 32 * part + 32, 1) for part in range(3)]
        last = jnp.where(lane < 32, moved[0], jnp.where(lane < 64, moved[1], moved[2]))
        grad[4 * group + 3] = last[:, 0:C]
        if group % 2:
            ready(group // 2)
    for tap in range(24, TAPS):
        grad[tap] = parts[(tap - 6) * C : (tap - 5) * C].astype(F32)[:, 0:C] * scale


PIECES = ((0, 8), (8, 16), (16, 24), (24, TAPS))


def sent(scale, parts, held, first, grads, sems):
    def piece(place, index):
        at = slice(*PIECES[index])
        return pltpu.make_async_copy(held.at[at], grads[place].at[at], sems.at[index])

    def ready(index):
        for place in range(2):

            @pl.when(first == place)
            def _():
                piece(place, index).start()

    unpack(scale, parts, held, ready)
    ready(3)
    for place in range(2):

        @pl.when(first == place)
        def _():
            for index in range(4):
                piece(place, index).wait()


def half_kernel(scale, parts, grad_one, grad_two, held, sems):
    sent(scale, parts, held, parities()[0], (grad_one, grad_two), sems)


def finish_kernel(
    scale, one_in, two_in, mine, other, grad_one, grad_two, grad_gain, grad_bias,
    held, sems, gain_line, bias_line, line_sems,
):
    core = parities()[0]
    last = slice(21 * C, HALF)
    rest = jnp.where(core == 1, mine[last].astype(F32), other[last].astype(F32)) * scale
    gain_line[...] = rest[0:1, 0:C]
    bias_line[...] = rest[1:2, 0:C]
    copies = started(((gain_line, grad_gain), (bias_line, grad_bias)), line_sems)
    sent(scale, other, held, core, (grad_two, grad_one), sems)
    for copy in copies:
        copy.wait()


def shape(dims, dtype):
    return jax.ShapeDtypeStruct(dims, dtype)


def dense_parts(features, cotangent, slots):
    return call(
        grid_kernel,
        (shape((2, SIDE, SIDE, SIDE, LANES), F32), shape((256, LANES), BF16), shape((256, LANES), BF16)),
        [HBM_SPEC] * 3,
        scratch=[
            pltpu.VMEM((4, 16, SIDE, LANES), F32),
            pltpu.SMEM(slots.shape, jnp.int32),
            pltpu.VMEM(features.shape, BF16),
            pltpu.VMEM(features.shape, BF16),
            pltpu.SemaphoreType.DMA((3,)),
        ],
        moved=2_000_000,
        name="dense_grid",
    )(*kept_far(slots, features, cotangent))


def rims(grid, far_x, near_x):
    return call(
        rim_kernel,
        (shape((384, LANES), BF16), shape((384, LANES), BF16)),
        [VMEM_SPEC] * 3,
        moved=1_500_000,
        name="rims",
    )(grid, far_x, near_x)


def weight_scratch():
    return [
        pltpu.VMEM((SPAN, LANES), BF16),
        pltpu.VMEM((LANES, SPAN), BF16),
        pltpu.VMEM((TAPS, C, C), BF16),
        pltpu.VMEM((TAPS, C, C), BF16),
    ]


def prepare(weight_one, weight_two, gain, bias):
    prepared = call(
        prepare_kernel,
        (shape((SPAN, LANES), BF16), shape((LANES, SPAN), BF16), shape((2, LANES), F32)),
        [HBM_SPEC] * 4,
        scratch=[
            pltpu.VMEM((TAPS, C, C), BF16),
            pltpu.VMEM((TAPS, C, C), BF16),
            pltpu.VMEM((1, C), F32),
            pltpu.VMEM((1, C), F32),
            pltpu.SemaphoreType.DMA((4,)),
        ],
        moved=3_000_000,
        name="prepare",
    )(*kept_far(weight_one, weight_two, gain.reshape(1, C), bias.reshape(1, C)))
    return [pltpu.with_memory_space_constraint(array, pltpu.VMEM) for array in prepared]


def gradients(grid, halos, rows, columns, gain_bias):
    return call(
        gradient_kernel,
        (shape((HALF, LANES), F32), shape((HALF, LANES), F32), shape((2 * RIM, LANES), BF16)),
        [VMEM_SPEC] * 8,
        scratch=[
            pltpu.VMEM((SIDE + 4, SIDE + 4, SIDE, LANES), F32),
            pltpu.VMEM((SIDE + 4, SIDE + 4, SIDE, 3 * LANES), F32),
            pltpu.VMEM((RIM, SPAN), BF16),
            pltpu.VMEM((LANES, SPAN), F32),
            pltpu.VMEM((LANES, SPAN), F32),
            pltpu.VMEM((2, HALF, LANES), F32),
        ],
        flops=2_400_000_000,
        moved=8_000_000,
        name="gradients",
        room=28,
    )(grid, *halos, rows, columns, gain_bias)


def outputs(slots, grid, inner, weight_one, weight_two):
    result = shape((4, 64, C), BF16)
    return call(
        output_kernel,
        (result, result),
        [SMEM_SPEC] + [VMEM_SPEC] * 2 + [HBM_SPEC] * 2,
        scratch=[
            pltpu.VMEM((SIDE + 2, SIDE + 2, SIDE, 3 * LANES), F32),
            pltpu.VMEM((OWN, SPAN), BF16),
            *weight_scratch(),
            pltpu.SemaphoreType.DMA((2,)),
        ],
        flops=900_000_000,
        moved=4_000_000,
        name="outputs",
        room=18,
    )(slots, grid, inner, *kept_far(weight_one, weight_two))


FAR_OUT = pl.BlockSpec(memory_space=pltpu.HBM)


def half_finished(mine, scale):
    grads = shape((TAPS, C, C), F32)
    return pl.pallas_call(
        functools.partial(half_kernel, scale),
        out_shape=(grads, grads),
        in_specs=[VMEM_SPEC],
        out_specs=(FAR_OUT, FAR_OUT),
        scratch_shapes=[pltpu.VMEM((TAPS, C, C), F32), pltpu.SemaphoreType.DMA((4,))],
        cost_estimate=pl.CostEstimate(flops=0, bytes_accessed=3_000_000, transcendentals=0),
        compiler_params=pltpu.CompilerParams(vmem_limit_bytes=8 << 20),
        name="half_finish",
    )(mine)


def finish(halves, mine, other, scale):
    grads, line = shape((TAPS, C, C), F32), shape((1, C), F32)
    return pl.pallas_call(
        functools.partial(finish_kernel, scale),
        out_shape=(grads, grads, line, line),
        in_specs=[HBM_SPEC, HBM_SPEC, VMEM_SPEC, VMEM_SPEC],
        out_specs=(FAR_OUT,) * 4,
        scratch_shapes=[
            pltpu.VMEM((TAPS, C, C), F32),
            pltpu.SemaphoreType.DMA((4,)),
            pltpu.VMEM((1, C), F32),
            pltpu.VMEM((1, C), F32),
            pltpu.SemaphoreType.DMA((2,)),
        ],
        input_output_aliases={0: 0, 1: 1},
        cost_estimate=pl.CostEstimate(flops=0, bytes_accessed=3_000_000, transcendentals=0),
        compiler_params=pltpu.CompilerParams(vmem_limit_bytes=8 << 20),
        name="finish",
    )(*halves, mine, other)


SIZES = dict(y=4, zh=4, core=2, zl=2, zp=2, x=4)
PLANE = ("y", "x", "zp")
LINE = ("zh", "zl")


def spread_out(block, axes):
    copies = jnp.broadcast_to(block, (lax.axis_size(axes),) + block.shape)
    return lax.all_to_all(copies, axes, 0, 0)


def other_core(block):
    return lax.ppermute(block, "core", [(0, 1), (1, 0)])


def reduce_all(keep, send, beside):
    pair = (keep + other_core(send)).astype(BF16)
    parts = lax.all_to_all(pair.reshape(lax.axis_size(PLANE), -1, LANES), PLANE, 0, 0)
    chunk = jnp.sum(parts.astype(F32), axis=0)
    chunks, beside = lax.optimization_barrier((spread_out(chunk, LINE), beside))
    chunk = jnp.sum(chunks, axis=0)
    return spread_out(chunk.astype(BF16), PLANE).reshape(HALF, LANES), beside


GX = ("y", "zh", "core")
GY = ("zl", "zp", "x")


def swapped(far, near, axis):
    count = lax.axis_size(axis)
    ends = {n: n + 1 for n in range(1, count - 1, 2)}
    route = [pair for low, high in ends.items() for pair in ((low, high), (high, low))]
    far = lax.ppermute(far, axis, route)
    near = lax.ppermute(near, axis, [(n, n ^ 1) for n in range(count)])
    return far, near


def body(features, cotangent, brick_slot, weight_one, weight_two, gain, bias):
    grid, far, near = dense_parts(features, cotangent, brick_slot)
    far, near, *given = lax.optimization_barrier((far, near, weight_one, weight_two, gain, bias))
    around_x = swapped(far, near, GX)
    around_x, prepared = lax.optimization_barrier((around_x, prepare(*given)))
    far, near = rims(grid, *around_x)
    halos = (*around_x, *swapped(far, near, GY))
    keep, send, inner = gradients(grid, halos, *prepared)
    out, grad = outputs(brick_slot, grid, inner, weight_one, weight_two)
    out, grad = out.reshape(features.shape), grad.reshape(features.shape)
    mine, (out, grad) = reduce_all(keep, send, (out, grad))
    other = other_core(mine)
    scale = 1.0 / math.sqrt(lax.axis_size(GX) * lax.axis_size(GY) * 256)
    halves = half_finished(mine, scale)
    grad_one, grad_two, grad_gain, grad_bias = finish(halves, mine, other, scale)
    return (
        out,
        grad,
        grad_one,
        grad_two,
        grad_gain.reshape(gain.shape),
        grad_bias.reshape(bias.shape),
    )


def solution(mesh):
    fine = jax.sharding.Mesh(mesh.devices.reshape(tuple(SIZES.values())), tuple(SIZES))
    slabs = P(GX, GY, None, None)
    in_specs = (slabs, slabs, P(GX, GY, None, None, None), P(), P(), P(), P())
    out_specs = (slabs, slabs, P(), P(), P(), P())
    return jax.shard_map(body, mesh=fine, in_specs=in_specs, out_specs=out_specs, check_vma=False)
```
